128 devices in a mesh: node: 32 (over z, y, core), local: 4 (over x).
Axes of the slice: x: 4, y: 4, z: 4, core: 2. Of those that a mesh axis runs over, the one named last changes fastest.
Arguments:
- tokens: bfloat16 [4096, 4096], P(('node', 'local')), may hold values from -6 to 6
- out_grad: bfloat16 [4096, 4096], P(('node', 'local')), may hold values from -6 to 6
- node_lists: int32 [4096, 4], P(('node', 'local')), may hold values from 0 to 31, as said below
- expert_local: int32 [4096, 8], P(('node', 'local')), may hold values from 0 to 15, as said below
- gate_fixed: int32 [4096, 8], P(('node', 'local')), may hold values from 4096 to 65535
- gate_weight: bfloat16 [128, 4096, 768], P(('node', 'local')), may hold values from -0.09375 to 0.09375
- up_weight: bfloat16 [128, 4096, 768], P(('node', 'local')), may hold values from -0.09375 to 0.09375
- down_weight: bfloat16 [128, 768, 4096], P(('node', 'local')), may hold values from -0.21875 to 0.21875
Outputs:
- token_grad: bfloat16 [4096, 4096], P(('node', 'local'))
- down_grad: bfloat16 [128, 768, 4096], P(('node', 'local'))
The draws below stay inside these ranges and needn't reach their ends.
Inputs may be any that keep to these rules, and one draw needn't show every extreme that they name: `node_lists`: each row holds 4 different group numbers. `expert_local`: each row holds 8 different numbers.
All inputs are finite; a program needn't handle non-finite values.
Results may differ from the reference program's by a relative error of at most 0.0064.
Values may be sent and summed in bfloat16 or wider, within the bound.
A program may use at most 128 MiB of HBM per device.

```python
import jax
import jax.numpy as jnp
from jax import lax

D = 4096
TOP = 8
FWIN = 768
NODE_LIM = 4
TOK_DEV = 32
NODES = 32
PER_NODE = 4
EXPERTS = 128
TOKENS = 4096
CAP = 2


def routing_pair(key):
    base = jax.random.fold_in(key, 11)
    subkeys = jax.random.split(base, 5)
    node_bias = jax.random.randint(subkeys[0], (NODES,), 0, 3 * 4096)
    node_noise = jax.random.randint(subkeys[1], (TOKENS, NODES), 0, 4 * 4096)
    hot_node = jax.random.randint(subkeys[2], (EXPERTS,), 0, NODES)
    hot_local = jax.random.randint(subkeys[3], (EXPERTS,), 0, PER_NODE)
    token_pos = jnp.arange(TOKENS, dtype=jnp.int32)
    block_of = token_pos // TOK_DEV
    forced = token_pos % TOK_DEV < CAP
    node_iota = jnp.arange(NODES, dtype=jnp.int32)[None, :]
    boost_node = jnp.where(forced[:, None] & (node_iota == hot_node[block_of][:, None]), 100000, 0)
    node_score = (node_noise + node_bias[None, :] + boost_node) * NODES + node_iota
    _, node_lists = lax.top_k(node_score, NODE_LIM)
    width_pick = NODE_LIM * PER_NODE
    pick_noise = jax.random.randint(subkeys[4], (TOKENS, width_pick), 0, 4096)
    pick_iota = jnp.arange(width_pick, dtype=jnp.int32)[None, :]
    boost_pick = jnp.where(forced[:, None] & (pick_iota == hot_local[block_of][:, None]), 100000, 0)
    pick_score = (pick_noise + boost_pick) * width_pick + pick_iota
    _, expert_local = lax.top_k(pick_score, TOP)
    return (node_lists.astype(jnp.int32), expert_local.astype(jnp.int32))


def draw_node_lists(key, part):
    return routing_pair(key)[0]


def draw_expert_local(key, part):
    return routing_pair(key)[1]


def with_ends(values, own_key, smallest, largest):
    index_at = [jax.random.randint(jax.random.fold_in(own_key, axis), (), 0, length) for axis, length in enumerate(values.shape)]
    widest = values.shape.index(max(values.shape))
    neighbour = index_at[:widest] + [(index_at[widest] + 1) % values.shape[widest]] + index_at[widest + 1:]
    return values.at[tuple(index_at)].set(smallest).at[tuple(neighbour)].set(largest)


def shard_levels(key, dims, cuts, low, top_value):
    level, own = 1.0, jax.random.fold_in(key, 6)
    for dim, shards_of in cuts:
        steps = jnp.exp(jax.random.uniform(jax.random.fold_in(own, dim), (shards_of,), jnp.float32, low / len(cuts), top_value / len(cuts)))
        level = level * jnp.repeat(steps, dims[dim] // shards_of).reshape([-1 if axis == dim else 1 for axis in range(len(dims))])
    return level


def gaussian(key, extent, scale, most, pieces=(), kind=jnp.bfloat16):
    level = shard_levels(key, extent, pieces, -0.22, 0.18) if pieces else 1.0
    array = jax.random.normal(key, extent, jnp.float32) * scale * level
    return jnp.minimum(jnp.maximum(array, -most), most).astype(kind)


def setup_inputs(seed: int = 0) -> dict:
    arg_keys = jax.random.split(jax.random.key(seed), 9)
    return {
        "tokens": gaussian(arg_keys[0], (TOKENS, D), 1.0, 6.0, ((0, 128),)),
        "out_grad": gaussian(arg_keys[1], (TOKENS, D), 1.0, 6.0, ((0, 128),)),
        "node_lists": draw_node_lists(jax.random.fold_in(arg_keys[8], 71), 0),
        "expert_local": draw_expert_local(jax.random.fold_in(arg_keys[8], 71), 0),
        "gate_fixed": with_ends(jax.random.randint(arg_keys[4], (TOKENS, TOP), 4096, 65536), jax.random.fold_in(arg_keys[4], 1), 4096, 65535).astype(jnp.int32),
        "gate_weight": gaussian(arg_keys[5], (EXPERTS, D, FWIN), D ** -0.5, 0.09375, ((0, 128),)),
        "up_weight": gaussian(arg_keys[6], (EXPERTS, D, FWIN), D ** -0.5, 0.09375, ((0, 128),)),
        "down_weight": gaussian(arg_keys[7], (EXPERTS, FWIN, D), FWIN ** -0.5, 0.21875, ((0, 128),)),
    }


def route_table(node_lists, expert_local):
    node_pick = jnp.take_along_axis(node_lists, (expert_local // PER_NODE).astype(jnp.int32), axis=1)
    expert_ids = (node_pick * PER_NODE + expert_local % PER_NODE).astype(jnp.int32)
    block_ids = expert_ids.reshape(EXPERTS, TOK_DEV * TOP)
    onehot = (block_ids[:, :, None] == jnp.arange(EXPERTS, dtype=jnp.int32)[None, None, :]).astype(jnp.int32)
    running = jnp.cumsum(onehot, axis=1)
    slot = jnp.sum(onehot * running, axis=2) - 1
    kept = slot < CAP
    source = jnp.arange(EXPERTS, dtype=jnp.int32)[:, None]
    position = jnp.where(kept, (block_ids * EXPERTS + source) * CAP + slot, EXPERTS * EXPERTS * CAP).astype(jnp.int32)
    assign_index = (source * (TOK_DEV * TOP) + jnp.arange(TOK_DEV * TOP, dtype=jnp.int32)[None, :]).astype(jnp.int32)
    table = jnp.full((EXPERTS * EXPERTS * CAP,), -1, jnp.int32)
    table = table.at[position.reshape(-1)].set(assign_index.reshape(-1), mode="drop")
    return table.reshape(EXPERTS, EXPERTS * CAP)


def reference(tokens, out_grad, node_lists, expert_local, gate_fixed, gate_weight, up_weight, down_weight):
    table = route_table(node_lists, expert_local)
    gate_flat = gate_fixed.reshape(-1)

    def one_expert(carry, inputs):
        assign, w_gate_e, w_up_e, w_down_e = inputs
        valid = assign >= 0
        safe = jnp.maximum(assign, 0).astype(jnp.int32)
        rows = (safe // TOP).astype(jnp.int32)
        x_rows = jnp.where(valid[:, None], tokens[rows], jnp.zeros((), jnp.bfloat16)).astype(jnp.bfloat16)
        gate_val = gate_flat[safe].astype(jnp.float32) * (1.0 / 65536.0)
        dy_rows = jnp.where(valid[:, None], gate_val[:, None] * out_grad[rows].astype(jnp.float32), jnp.float32(0.0)).astype(jnp.bfloat16)
        gate_act = jnp.dot(x_rows, w_gate_e, preferred_element_type=jnp.float32)
        up_act = jnp.dot(x_rows, w_up_e, preferred_element_type=jnp.float32)
        sig = jax.nn.sigmoid(gate_act)
        hidden = (gate_act * sig * up_act).astype(jnp.bfloat16)
        down_g = lax.dot_general(hidden, dy_rows, (((0,), (0,)), ((), ())), preferred_element_type=jnp.float32).astype(jnp.bfloat16)
        hidden_grad = jnp.dot(dy_rows, w_down_e.T, preferred_element_type=jnp.float32)
        gate_grad = (hidden_grad * up_act * sig * (1.0 + gate_act * (1.0 - sig))).astype(jnp.bfloat16)
        up_grad = (hidden_grad * gate_act * sig).astype(jnp.bfloat16)
        row_grad = (jnp.dot(gate_grad, w_gate_e.T, preferred_element_type=jnp.float32)
                    + jnp.dot(up_grad, w_up_e.T, preferred_element_type=jnp.float32)).astype(jnp.bfloat16)
        row_grad = lax.optimization_barrier(row_grad)
        added = jnp.where(valid[:, None], row_grad.astype(jnp.float32), jnp.float32(0.0))
        carry = carry.at[rows].add(added)
        return carry, down_g

    start = jnp.zeros((TOKENS, D), jnp.float32)
    total, down_grad = lax.scan(one_expert, start, (table, gate_weight, up_weight, down_weight))
    return total.astype(jnp.bfloat16), down_grad
```

```python
import functools
import jax
import jax.numpy as jnp
from jax import lax
from jax.sharding import PartitionSpec as P
from jax.experimental import pallas as pl
from jax.experimental.pallas import tpu as pltpu


def _exchange_kernel(n_local, *refs):
    count = (len(refs) - 2) // 2
    srcs = refs[:count]
    dsts = refs[count:2 * count]
    send_sems = refs[2 * count]
    recv_sems = refs[2 * count + 1]
    node = lax.axis_index("node")
    local = lax.axis_index("local")
    me = node * n_local + local
    devices = lax.axis_size("node") * n_local
    rows = srcs[0].shape[0] // devices

    def copy_to(p, i):
        return pltpu.make_async_remote_copy(
            src_ref=srcs[i].at[pl.ds(p * rows, rows)],
            dst_ref=dsts[i].at[pl.ds(me * rows, rows)],
            send_sem=send_sems.at[i],
            recv_sem=recv_sems.at[i],
            device_id=(p // n_local, p % n_local),
            device_id_type=pl.DeviceIdType.MESH,
        )

    def local_copy(i):
        return pltpu.make_async_copy(
            srcs[i].at[pl.ds(me * rows, rows)],
            dsts[i].at[pl.ds(me * rows, rows)],
            recv_sems.at[i],
        )

    for i in range(count):
        local_copy(i).start()

    def start_body(step, carry):
        p = lax.rem(me + step, devices)
        for i in range(count):
            copy_to(p, i).start()
        return carry

    lax.fori_loop(1, devices, start_body, 0)
    nxt = lax.rem(me + 1, devices)
    for i in range(count):
        pltpu.make_async_copy(dsts[i], dsts[i], recv_sems.at[i]).wait()
        pltpu.make_async_remote_copy(
            src_ref=srcs[i].at[pl.ds(0, (devices - 1) * rows)],
            dst_ref=dsts[i].at[pl.ds(0, (devices - 1) * rows)],
            send_sem=send_sems.at[i],
            recv_sem=recv_sems.at[i],
            device_id=(nxt // n_local, nxt % n_local),
            device_id_type=pl.DeviceIdType.MESH,
        ).wait_send()


def exchange(*arrays):
    n_local = lax.axis_size("local")
    count = len(arrays)
    return pl.pallas_call(
        functools.partial(_exchange_kernel, n_local),
        out_shape=[jax.ShapeDtypeStruct(a.shape, a.dtype) for a in arrays],
        in_specs=[pl.BlockSpec(memory_space=pl.ANY)] * count,
        out_specs=[pl.BlockSpec(memory_space=pl.ANY)] * count,
        scratch_shapes=[
            pltpu.SemaphoreType.DMA((count,)),
            pltpu.SemaphoreType.DMA((count,)),
        ],
        compiler_params=pltpu.CompilerParams(has_side_effects=True),
    )(*arrays)


def expert_math(x_rows, dy_rows, w_gate_e, w_up_e, w_down_e):
    gate_act = jnp.dot(x_rows, w_gate_e, preferred_element_type=jnp.float32)
    up_act = jnp.dot(x_rows, w_up_e, preferred_element_type=jnp.float32)
    sig = jax.nn.sigmoid(gate_act)
    hidden = (gate_act * sig * up_act).astype(jnp.bfloat16)
    contract_rows = (((0,), (0,)), ((), ()))
    contract_last = (((1,), (1,)), ((), ()))
    down_local = lax.dot_general(
        hidden, dy_rows, contract_rows, preferred_element_type=jnp.float32
    ).astype(jnp.bfloat16)
    hidden_grad = lax.dot_general(
        dy_rows, w_down_e, contract_last, preferred_element_type=jnp.float32
    )
    gate_grad = (hidden_grad * up_act * sig * (1.0 + gate_act * (1.0 - sig))).astype(jnp.bfloat16)
    up_grad = (hidden_grad * gate_act * sig).astype(jnp.bfloat16)
    row_grad = (
        lax.dot_general(gate_grad, w_gate_e, contract_last, preferred_element_type=jnp.float32)
        + lax.dot_general(up_grad, w_up_e, contract_last, preferred_element_type=jnp.float32)
    ).astype(jnp.bfloat16)
    return (down_local, row_grad)


def body(
    tokens, out_grad, node_lists, expert_local, gate_fixed, gate_weight, up_weight, down_weight
):
    nodes = lax.axis_size("node")
    per_node = lax.axis_size("local")
    experts = nodes * per_node
    tok_dev, top_count = expert_local.shape
    width = tokens.shape[1]
    capacity = tok_dev * top_count // experts
    node_pick = jnp.take_along_axis(node_lists, expert_local // per_node, axis=1)
    expert_ids = (node_pick * per_node + expert_local % per_node).reshape(-1)
    onehot = (expert_ids[:, None] == jnp.arange(experts, dtype=jnp.int32)[None, :]).astype(
        jnp.int32
    )
    running = jnp.cumsum(onehot, axis=0)
    slot = jnp.sum(onehot * running, axis=1) - 1
    kept = slot < capacity
    position = jnp.where(kept, expert_ids * capacity + slot, experts * capacity)
    w_gate_e = gate_weight[0]
    w_up_e = up_weight[0]
    w_down_e = down_weight[0]
    gate_flat = gate_fixed.reshape(-1)
    table = jnp.full((experts * capacity,), -1, jnp.int32)
    table = table.at[position].set(jnp.arange(tok_dev * top_count, dtype=jnp.int32), mode="drop")
    valid = table >= 0
    safe = jnp.maximum(table, 0)
    rows = safe // top_count
    send_x = jnp.where(valid[:, None], tokens[rows], jnp.zeros((), jnp.bfloat16))
    gate_val = gate_flat[safe].astype(jnp.float32) * (1.0 / 65536.0)
    send_dy = jnp.where(valid[:, None], gate_val[:, None] * out_grad[rows].astype(jnp.float32), 0.0)
    send_dy = send_dy.astype(jnp.bfloat16)
    tile_rows = 8
    flat = (experts * tile_rows, capacity * width // tile_rows)
    x_rows, dy_rows = exchange(send_x.reshape(flat), send_dy.reshape(flat))
    x_rows = x_rows.reshape(experts * capacity, width)
    dy_rows = dy_rows.reshape(experts * capacity, width)
    down_local, row_grad = expert_math(x_rows, dy_rows, w_gate_e, w_up_e, w_down_e)
    (returned,) = exchange(row_grad.reshape(flat))
    returned = returned.reshape(experts * capacity, width)
    lookup = jnp.where(kept, position, 0)
    picked = jnp.where(kept[:, None], returned[lookup].astype(jnp.float32), 0.0)
    token_grad = jnp.sum(picked.reshape(tok_dev, top_count, width), axis=1).astype(jnp.bfloat16)
    return (token_grad, down_local[None])


def solution(mesh):
    return jax.shard_map(
        body,
        mesh=mesh,
        in_specs=(
            P(("node", "local"), None),
            P(("node", "local"), None),
            P(("node", "local"), None),
            P(("node", "local"), None),
            P(("node", "local"), None),
            P(("node", "local"), None, None),
            P(("node", "local"), None, None),
            P(("node", "local"), None, None),
        ),
        out_specs=(P(("node", "local"), None), P(("node", "local"), None, None)),
        check_vma=False,
    )
```

```python
import functools
import jax
import jax.numpy as jnp
from jax import lax
from jax.sharding import PartitionSpec as P
from jax.experimental import pallas as pl
from jax.experimental.pallas import tpu as pltpu


def _exchange_kernel(n_local, *refs):
    count = (len(refs) - 2) // 2
    srcs = refs[:count]
    dsts = refs[count:2 * count]
    send_sems = refs[2 * count]
    recv_sems = refs[2 * count + 1]
    node = lax.axis_index("node")
    local = lax.axis_index("local")
    me = node * n_local + local
    devices = lax.axis_size("node") * n_local
    rows = srcs[0].shape[0] // devices

    def copy_to(p, i):
        return pltpu.make_async_remote_copy(
            src_ref=srcs[i].at[pl.ds(p * rows, rows)],
            dst_ref=dsts[i].at[pl.ds(me * rows, rows)],
            send_sem=send_sems.at[i],
            recv_sem=recv_sems.at[i],
            device_id=(p // n_local, p % n_local),
            device_id_type=pl.DeviceIdType.MESH,
        )

    def local_copy(i):
        return pltpu.make_async_copy(
            srcs[i].at[pl.ds(me * rows, rows)],
            dsts[i].at[pl.ds(me * rows, rows)],
            recv_sems.at[i],
        )

    for i in range(count):
        local_copy(i).start()

    core = node % 2
    y_pos = (node // 2) % 4
    z_pos = node // 8

    def start_body(step, carry):
        t = step % 64
        d_core = step // 64
        dx = t % 4
        dy = (t // 4 + dx) % 4
        dz = (t // 16 + t // 4 + dx) % 4
        node_to = (((z_pos + dz) % 4) * 4 + (y_pos + dy) % 4) * 2 + (core + d_core) % 2
        p = node_to * n_local + (local + dx) % 4
        for i in range(count):
            copy_to(p, i).start()
        return carry

    lax.fori_loop(1, devices, start_body, 0)
    nxt = lax.rem(me + 1, devices)
    for i in range(count):
        pltpu.make_async_copy(dsts[i], dsts[i], recv_sems.at[i]).wait()
        pltpu.make_async_remote_copy(
            src_ref=srcs[i].at[pl.ds(0, (devices - 1) * rows)],
            dst_ref=dsts[i].at[pl.ds(0, (devices - 1) * rows)],
            send_sem=send_sems.at[i],
            recv_sem=recv_sems.at[i],
            device_id=(nxt // n_local, nxt % n_local),
            device_id_type=pl.DeviceIdType.MESH,
        ).wait_send()


def exchange(*arrays):
    n_local = lax.axis_size("local")
    count = len(arrays)
    return pl.pallas_call(
        functools.partial(_exchange_kernel, n_local),
        out_shape=[jax.ShapeDtypeStruct(a.shape, a.dtype) for a in arrays],
        in_specs=[pl.BlockSpec(memory_space=pl.ANY)] * count,
        out_specs=[pl.BlockSpec(memory_space=pl.ANY)] * count,
        scratch_shapes=[
            pltpu.SemaphoreType.DMA((count,)),
            pltpu.SemaphoreType.DMA((count,)),
        ],
        compiler_params=pltpu.CompilerParams(has_side_effects=True),
    )(*arrays)


def expert_math(x_rows, dy_rows, w_gate_e, w_up_e, w_down_e):
    gate_act = jnp.dot(x_rows, w_gate_e, preferred_element_type=jnp.float32)
    up_act = jnp.dot(x_rows, w_up_e, preferred_element_type=jnp.float32)
    sig = jax.nn.sigmoid(gate_act)
    hidden = (gate_act * sig * up_act).astype(jnp.bfloat16)
    contract_rows = (((0,), (0,)), ((), ()))
    contract_last = (((1,), (1,)), ((), ()))
    down_local = lax.dot_general(
        hidden, dy_rows, contract_rows, preferred_element_type=jnp.float32
    ).astype(jnp.bfloat16)
    hidden_grad = lax.dot_general(
        dy_rows, w_down_e, contract_last, preferred_element_type=jnp.float32
    )
    gate_grad = (hidden_grad * up_act * sig * (1.0 + gate_act * (1.0 - sig))).astype(jnp.bfloat16)
    up_grad = (hidden_grad * gate_act * sig).astype(jnp.bfloat16)
    row_grad = (
        lax.dot_general(gate_grad, w_gate_e, contract_last, preferred_element_type=jnp.float32)
        + lax.dot_general(up_grad, w_up_e, contract_last, preferred_element_type=jnp.float32)
    ).astype(jnp.bfloat16)
    return (down_local, row_grad)


def body(
    tokens, out_grad, node_lists, expert_local, gate_fixed, gate_weight, up_weight, down_weight
):
    nodes = lax.axis_size("node")
    per_node = lax.axis_size("local")
    experts = nodes * per_node
    tok_dev, top_count = expert_local.shape
    width = tokens.shape[1]
    capacity = tok_dev * top_count // experts
    node_pick = jnp.take_along_axis(node_lists, expert_local // per_node, axis=1)
    expert_ids = (node_pick * per_node + expert_local % per_node).reshape(-1)
    onehot = (expert_ids[:, None] == jnp.arange(experts, dtype=jnp.int32)[None, :]).astype(
        jnp.int32
    )
    running = jnp.cumsum(onehot, axis=0)
    slot = jnp.sum(onehot * running, axis=1) - 1
    kept = slot < capacity
    position = jnp.where(kept, expert_ids * capacity + slot, experts * capacity)
    w_gate_e = gate_weight[0]
    w_up_e = up_weight[0]
    w_down_e = down_weight[0]
    gate_flat = gate_fixed.reshape(-1)
    table = jnp.full((experts * capacity,), -1, jnp.int32)
    table = table.at[position].set(jnp.arange(tok_dev * top_count, dtype=jnp.int32), mode="drop")
    valid = table >= 0
    safe = jnp.maximum(table, 0)
    rows = safe // top_count
    send_x = jnp.where(valid[:, None], tokens[rows], jnp.zeros((), jnp.bfloat16))
    gate_val = gate_flat[safe].astype(jnp.float32) * (1.0 / 65536.0)
    send_dy = jnp.where(valid[:, None], gate_val[:, None] * out_grad[rows].astype(jnp.float32), 0.0)
    send_dy = send_dy.astype(jnp.bfloat16)
    tile_rows = 8
    flat = (experts * tile_rows, capacity * width // tile_rows)
    x_rows, dy_rows = exchange(send_x.reshape(flat), send_dy.reshape(flat))
    x_rows = x_rows.reshape(experts * capacity, width)
    dy_rows = dy_rows.reshape(experts * capacity, width)
    down_local, row_grad = expert_math(x_rows, dy_rows, w_gate_e, w_up_e, w_down_e)
    (returned,) = exchange(row_grad.reshape(flat))
    returned = returned.reshape(experts * capacity, width)
    lookup = jnp.where(kept, position, 0)
    picked = jnp.where(kept[:, None], returned[lookup].astype(jnp.float32), 0.0)
    token_grad = jnp.sum(picked.reshape(tok_dev, top_count, width), axis=1).astype(jnp.bfloat16)
    return (token_grad, down_local[None])


def solution(mesh):
    return jax.shard_map(
        body,
        mesh=mesh,
        in_specs=(
            P(("node", "local"), None),
            P(("node", "local"), None),
            P(("node", "local"), None),
            P(("node", "local"), None),
            P(("node", "local"), None),
            P(("node", "local"), None, None),
            P(("node", "local"), None, None),
            P(("node", "local"), None, None),
        ),
        out_specs=(P(("node", "local"), None), P(("node", "local"), None, None)),
        check_vma=False,
    )
```

```python
import jax
import jax.numpy as jnp
from jax import lax
from jax.sharding import PartitionSpec as P


def expert_math(x_rows, dy_rows, w_gate_e, w_up_e, w_down_e):
    gate_act = jnp.einsum("psd,dh->psh", x_rows, w_gate_e, preferred_element_type=jnp.float32)
    up_act = jnp.einsum("psd,dh->psh", x_rows, w_up_e, preferred_element_type=jnp.float32)
    sig = jax.nn.sigmoid(gate_act)
    hidden = (gate_act * sig * up_act).astype(jnp.bfloat16)
    down_local = jnp.einsum(
        "psh,psd->hd", hidden, dy_rows, preferred_element_type=jnp.float32
    ).astype(jnp.bfloat16)
    hidden_grad = jnp.einsum("psd,hd->psh", dy_rows, w_down_e, preferred_element_type=jnp.float32)
    gate_grad = (hidden_grad * up_act * sig * (1.0 + gate_act * (1.0 - sig))).astype(jnp.bfloat16)
    up_grad = (hidden_grad * gate_act * sig).astype(jnp.bfloat16)
    row_grad = (
        jnp.einsum("psh,dh->psd", gate_grad, w_gate_e, preferred_element_type=jnp.float32)
        + jnp.einsum("psh,dh->psd", up_grad, w_up_e, preferred_element_type=jnp.float32)
    ).astype(jnp.bfloat16)
    return (down_local, row_grad)


def body(
    tokens, out_grad, node_lists, expert_local, gate_fixed, gate_weight, up_weight, down_weight
):
    nodes = lax.axis_size("node")
    per_node = lax.axis_size("local")
    experts = nodes * per_node
    tok_dev, top_count = expert_local.shape
    width = tokens.shape[1]
    capacity = tok_dev * top_count // experts
    node_pick = jnp.take_along_axis(node_lists, expert_local // per_node, axis=1)
    expert_ids = (node_pick * per_node + expert_local % per_node).reshape(-1)
    onehot = (expert_ids[:, None] == jnp.arange(experts, dtype=jnp.int32)[None, :]).astype(
        jnp.int32
    )
    running = jnp.cumsum(onehot, axis=0)
    slot = jnp.sum(onehot * running, axis=1) - 1
    kept = slot < capacity
    position = jnp.where(kept, expert_ids * capacity + slot, experts * capacity)
    w_gate_e = gate_weight[0]
    w_up_e = up_weight[0]
    w_down_e = down_weight[0]
    gate_flat = gate_fixed.reshape(-1)
    table = jnp.full((experts * capacity,), -1, jnp.int32)
    table = table.at[position].set(jnp.arange(tok_dev * top_count, dtype=jnp.int32), mode="drop")
    valid = table >= 0
    safe = jnp.maximum(table, 0)
    rows = safe // top_count
    x_sel = jnp.where(valid[:, None], tokens[rows], jnp.zeros((), jnp.bfloat16))
    gate_val = gate_flat[safe].astype(jnp.float32) * (1.0 / 65536.0)
    dy_sel = (gate_val[:, None] * out_grad[rows].astype(jnp.float32)).astype(jnp.bfloat16)
    dy_sel = jnp.where(valid[:, None], dy_sel, jnp.zeros((), jnp.bfloat16))
    send_x = x_sel.reshape(experts, capacity, width)
    send_dy = dy_sel.reshape(experts, capacity, width)
    recv_x = lax.all_to_all(send_x, ("node", "local"), split_axis=0, concat_axis=0, tiled=True)
    recv_dy = lax.all_to_all(send_dy, ("node", "local"), split_axis=0, concat_axis=0, tiled=True)
    down_local, row_grad = expert_math(recv_x, recv_dy, w_gate_e, w_up_e, w_down_e)
    returned = lax.all_to_all(row_grad, ("node", "local"), split_axis=0, concat_axis=0, tiled=True)
    returned = returned.reshape(experts * capacity, width)
    lookup = jnp.where(kept, position, 0)
    picked = jnp.where(kept[:, None], returned[lookup].astype(jnp.float32), 0.0)
    token_grad = jnp.sum(picked.reshape(tok_dev, top_count, width), axis=1).astype(jnp.bfloat16)
    return (token_grad, down_local[None])


def solution(mesh):
    return jax.shard_map(
        body,
        mesh=mesh,
        in_specs=(
            P(("node", "local"), None),
            P(("node", "local"), None),
            P(("node", "local"), None),
            P(("node", "local"), None),
            P(("node", "local"), None),
            P(("node", "local"), None, None),
            P(("node", "local"), None, None),
            P(("node", "local"), None, None),
        ),
        out_specs=(P(("node", "local"), None), P(("node", "local"), None, None)),
        check_vma=False,
    )
```

```python
import functools
import jax
import jax.numpy as jnp
from jax import lax
from jax.sharding import PartitionSpec as P
from jax.experimental import pallas as pl
from jax.experimental.pallas import tpu as pltpu


def _exchange_kernel(n_local, *refs):
    count = (len(refs) - 2) // 2
    srcs = refs[:count]
    dsts = refs[count:2 * count]
    send_sems = refs[2 * count]
    recv_sems = refs[2 * count + 1]
    node = lax.axis_index("node")
    local = lax.axis_index("local")
    me = node * n_local + local
    devices = lax.axis_size("node") * n_local
    rows = srcs[0].shape[0] // devices

    def copy_to(p, i):
        return pltpu.make_async_remote_copy(
            src_ref=srcs[i].at[pl.ds(p * rows, rows)],
            dst_ref=dsts[i].at[pl.ds(me * rows, rows)],
            send_sem=send_sems.at[i],
            recv_sem=recv_sems.at[i],
            device_id=(p // n_local, p % n_local),
            device_id_type=pl.DeviceIdType.MESH,
        )

    def local_copy(i):
        return pltpu.make_async_copy(
            srcs[i].at[pl.ds(me * rows, rows)],
            dsts[i].at[pl.ds(me * rows, rows)],
            recv_sems.at[i],
        )

    for i in range(count):
        local_copy(i).start()

    core = node % 2
    y_pos = (node // 2) % 4
    z_pos = node // 8

    def start_body(step, carry):
        t = step % 64
        d_core = step // 64
        dx = t % 4
        dy = (t // 4 + dx) % 4
        dz = (t // 16 + t // 4 + dx) % 4
        node_to = (((z_pos + dz) % 4) * 4 + (y_pos + dy) % 4) * 2 + (core + d_core) % 2
        p = node_to * n_local + (local + dx) % 4
        for i in range(count):
            copy_to(p, i).start()
        return carry

    lax.fori_loop(1, devices, start_body, 0)
    nxt = lax.rem(me + 1, devices)
    for i in range(count):
        pltpu.make_async_copy(dsts[i], dsts[i], recv_sems.at[i]).wait()
        pltpu.make_async_remote_copy(
            src_ref=srcs[i].at[pl.ds(0, (devices - 1) * rows)],
            dst_ref=dsts[i].at[pl.ds(0, (devices - 1) * rows)],
            send_sem=send_sems.at[i],
            recv_sem=recv_sems.at[i],
            device_id=(nxt // n_local, nxt % n_local),
            device_id_type=pl.DeviceIdType.MESH,
        ).wait_send()


def exchange(*arrays):
    n_local = lax.axis_size("local")
    count = len(arrays)
    return pl.pallas_call(
        functools.partial(_exchange_kernel, n_local),
        out_shape=[jax.ShapeDtypeStruct(a.shape, a.dtype) for a in arrays],
        in_specs=[pl.BlockSpec(memory_space=pl.ANY)] * count,
        out_specs=[pl.BlockSpec(memory_space=pl.ANY)] * count,
        scratch_shapes=[
            pltpu.SemaphoreType.DMA((count,)),
            pltpu.SemaphoreType.DMA((count,)),
        ],
        compiler_params=pltpu.CompilerParams(has_side_effects=True),
    )(*arrays)


def expert_math(x_rows, dy_rows, w_gate_e, w_up_e, w_down_e):
    gate_act = jnp.dot(x_rows, w_gate_e, preferred_element_type=jnp.float32)
    up_act = jnp.dot(x_rows, w_up_e, preferred_element_type=jnp.float32)
    sig = jax.nn.sigmoid(gate_act)
    hidden = (gate_act * sig * up_act).astype(jnp.bfloat16)
    contract_rows = (((0,), (0,)), ((), ()))
    contract_last = (((1,), (1,)), ((), ()))
    down_local = lax.dot_general(
        hidden, dy_rows, contract_rows, preferred_element_type=jnp.float32
    ).astype(jnp.bfloat16)
    hidden_grad = lax.dot_general(
        dy_rows, w_down_e, contract_last, preferred_element_type=jnp.float32
    )
    gate_grad = (hidden_grad * up_act * sig * (1.0 + gate_act * (1.0 - sig))).astype(jnp.bfloat16)
    up_grad = (hidden_grad * gate_act * sig).astype(jnp.bfloat16)
    row_grad = (
        lax.dot_general(gate_grad, w_gate_e, contract_last, preferred_element_type=jnp.float32)
        + lax.dot_general(up_grad, w_up_e, contract_last, preferred_element_type=jnp.float32)
    ).astype(jnp.bfloat16)
    return (down_local, row_grad)


def body(
    tokens, out_grad, node_lists, expert_local, gate_fixed, gate_weight, up_weight, down_weight
):
    nodes = lax.axis_size("node")
    per_node = lax.axis_size("local")
    experts = nodes * per_node
    tok_dev, top_count = expert_local.shape
    width = tokens.shape[1]
    capacity = tok_dev * top_count // experts
    node_pick = jnp.take_along_axis(node_lists, expert_local // per_node, axis=1)
    expert_ids = (node_pick * per_node + expert_local % per_node).reshape(-1)
    onehot = (expert_ids[:, None] == jnp.arange(experts, dtype=jnp.int32)[None, :]).astype(
        jnp.int32
    )
    running = jnp.cumsum(onehot, axis=0)
    slot = jnp.sum(onehot * running, axis=1) - 1
    kept = slot < capacity
    position = jnp.where(kept, expert_ids * capacity + slot, experts * capacity)
    w_gate_e = gate_weight[0]
    w_up_e = up_weight[0]
    w_down_e = down_weight[0]
    gate_flat = gate_fixed.reshape(-1)
    table = jnp.full((experts * capacity,), -1, jnp.int32)
    table = table.at[position].set(jnp.arange(tok_dev * top_count, dtype=jnp.int32), mode="drop")
    valid = table >= 0
    safe = jnp.maximum(table, 0)
    rows = safe // top_count
    tile_rows = 8
    blocks = tile_rows // capacity
    piece = width // blocks
    holds = valid[:, None] & (rows[:, None] == jnp.arange(tok_dev, dtype=jnp.int32)[None, :])
    same_block = jnp.eye(blocks, dtype=jnp.bool_)
    select = (holds[:, None, :, None] & same_block[None, :, None, :]).reshape(
        experts * tile_rows, tok_dev * blocks
    ).astype(jnp.bfloat16)
    tok_pieces = tokens.reshape(tok_dev * blocks, piece)
    og_pieces = out_grad.reshape(tok_dev * blocks, piece)
    send_x = jnp.dot(select, tok_pieces, preferred_element_type=jnp.float32).astype(jnp.bfloat16)
    gate_val = jnp.where(valid, gate_flat[safe].astype(jnp.float32) * (1.0 / 65536.0), 0.0)
    gate_rows = jnp.repeat(gate_val, blocks)
    og_sel = jnp.dot(select, og_pieces, preferred_element_type=jnp.float32)
    send_dy = (gate_rows[:, None] * og_sel).astype(jnp.bfloat16)
    x_flat, dy_flat = exchange(send_x, send_dy)
    x_rows = x_flat.reshape(experts * capacity, width)
    dy_rows = dy_flat.reshape(experts * capacity, width)
    down_local, row_grad = expert_math(x_rows, dy_rows, w_gate_e, w_up_e, w_down_e)
    (returned,) = exchange(row_grad.reshape(experts * tile_rows, piece))
    total = jnp.dot(select.T, returned, preferred_element_type=jnp.float32)
    token_grad = total.reshape(tok_dev, width).astype(jnp.bfloat16)
    return (token_grad, down_local[None])


def solution(mesh):
    return jax.shard_map(
        body,
        mesh=mesh,
        in_specs=(
            P(("node", "local"), None),
            P(("node", "local"), None),
            P(("node", "local"), None),
            P(("node", "local"), None),
            P(("node", "local"), None),
            P(("node", "local"), None, None),
            P(("node", "local"), None, None),
            P(("node", "local"), None, None),
        ),
        out_specs=(P(("node", "local"), None), P(("node", "local"), None, None)),
        check_vma=False,
    )
```

```python
import functools
import jax
import jax.numpy as jnp
from jax import lax
from jax.sharding import PartitionSpec as P
from jax.experimental import pallas as pl
from jax.experimental.pallas import tpu as pltpu


def _exchange_kernel(n_local, *refs):
    count = (len(refs) - 2) // 2
    srcs = refs[:count]
    dsts = refs[count:2 * count]
    send_sems = refs[2 * count]
    recv_sems = refs[2 * count + 1]
    node = lax.axis_index("node")
    local = lax.axis_index("local")
    me = node * n_local + local
    devices = lax.axis_size("node") * n_local
    rows = srcs[0].shape[0] // devices

    def copy_to(p, i):
        return pltpu.make_async_remote_copy(
            src_ref=srcs[i].at[pl.ds(p * rows, rows)],
            dst_ref=dsts[i].at[pl.ds(me * rows, rows)],
            send_sem=send_sems.at[i],
            recv_sem=recv_sems.at[i],
            device_id=(p // n_local, p % n_local),
            device_id_type=pl.DeviceIdType.MESH,
        )

    def local_copy(i):
        return pltpu.make_async_copy(
            srcs[i].at[pl.ds(me * rows, rows)],
            dsts[i].at[pl.ds(me * rows, rows)],
            recv_sems.at[i],
        )

    for i in range(count):
        local_copy(i).start()

    core = node % 2
    y_pos = (node // 2) % 4
    z_pos = node // 8

    def start_body(step, carry):
        t = step % 64
        d_core = step // 64
        dx = t % 4
        dy = (t // 4 + dx) % 4
        dz = (t // 16 + t // 4 + dx) % 4
        node_to = (((z_pos + dz) % 4) * 4 + (y_pos + dy) % 4) * 2 + (core + d_core) % 2
        p = node_to * n_local + (local + dx) % 4
        for i in range(count):
            copy_to(p, i).start()
        return carry

    lax.fori_loop(1, devices, start_body, 0)
    nxt = lax.rem(me + 1, devices)
    for i in range(count):
        pltpu.make_async_copy(dsts[i], dsts[i], recv_sems.at[i]).wait()
        pltpu.make_async_remote_copy(
            src_ref=srcs[i].at[pl.ds(0, (devices - 1) * rows)],
            dst_ref=dsts[i].at[pl.ds(0, (devices - 1) * rows)],
            send_sem=send_sems.at[i],
            recv_sem=recv_sems.at[i],
            device_id=(nxt // n_local, nxt % n_local),
            device_id_type=pl.DeviceIdType.MESH,
        ).wait_send()


def exchange(*arrays):
    n_local = lax.axis_size("local")
    count = len(arrays)
    return pl.pallas_call(
        functools.partial(_exchange_kernel, n_local),
        out_shape=[jax.ShapeDtypeStruct(a.shape, a.dtype) for a in arrays],
        in_specs=[pl.BlockSpec(memory_space=pl.ANY)] * count,
        out_specs=[pl.BlockSpec(memory_space=pl.ANY)] * count,
        scratch_shapes=[
            pltpu.SemaphoreType.DMA((count,)),
            pltpu.SemaphoreType.DMA((count,)),
        ],
        compiler_params=pltpu.CompilerParams(has_side_effects=True),
    )(*arrays)


def expert_math(x_rows, dy_rows, w_gate_e, w_up_e, w_down_e):
    gate_act = jnp.dot(x_rows, w_gate_e, preferred_element_type=jnp.float32)
    up_act = jnp.dot(x_rows, w_up_e, preferred_element_type=jnp.float32)
    sig = jax.nn.sigmoid(gate_act)
    hidden = (gate_act * sig * up_act).astype(jnp.bfloat16)
    contract_rows = (((0,), (0,)), ((), ()))
    contract_last = (((1,), (1,)), ((), ()))
    down_local = lax.dot_general(
        hidden, dy_rows, contract_rows, preferred_element_type=jnp.float32
    ).astype(jnp.bfloat16)
    hidden_grad = lax.dot_general(
        dy_rows, w_down_e, contract_last, preferred_element_type=jnp.float32
    )
    gate_grad = (hidden_grad * up_act * sig * (1.0 + gate_act * (1.0 - sig))).astype(jnp.bfloat16)
    up_grad = (hidden_grad * gate_act * sig).astype(jnp.bfloat16)
    row_grad = (
        lax.dot_general(gate_grad, w_gate_e, contract_last, preferred_element_type=jnp.float32)
        + lax.dot_general(up_grad, w_up_e, contract_last, preferred_element_type=jnp.float32)
    ).astype(jnp.bfloat16)
    return (down_local, row_grad)


def body(
    tokens, out_grad, node_lists, expert_local, gate_fixed, gate_weight, up_weight, down_weight
):
    nodes = lax.axis_size("node")
    per_node = lax.axis_size("local")
    experts = nodes * per_node
    tok_dev, top_count = expert_local.shape
    width = tokens.shape[1]
    capacity = tok_dev * top_count // experts
    node_pick = jnp.take_along_axis(node_lists, expert_local // per_node, axis=1)
    expert_ids = (node_pick * per_node + expert_local % per_node).reshape(-1)
    onehot = (expert_ids[:, None] == jnp.arange(experts, dtype=jnp.int32)[None, :]).astype(
        jnp.int32
    )
    running = jnp.cumsum(onehot, axis=0)
    slot = jnp.sum(onehot * running, axis=1) - 1
    kept = slot < capacity
    position = jnp.where(kept, expert_ids * capacity + slot, experts * capacity)
    w_gate_e = gate_weight[0]
    w_up_e = up_weight[0]
    w_down_e = down_weight[0]
    gate_flat = gate_fixed.reshape(-1)
    table = jnp.full((experts * capacity,), -1, jnp.int32)
    table = table.at[position].set(jnp.arange(tok_dev * top_count, dtype=jnp.int32), mode="drop")
    valid = table >= 0
    safe = jnp.maximum(table, 0)
    rows = safe // top_count
    tile_rows = 8
    blocks = tile_rows // capacity
    piece = width // blocks
    slot_token = jnp.where(valid, rows, -1)
    row_key = jnp.where(
        jnp.repeat(valid, blocks),
        jnp.repeat(slot_token, blocks) * blocks + jnp.arange(experts * tile_rows, dtype=jnp.int32) % blocks,
        -1,
    )
    select = (
        row_key[:, None] == jnp.arange(tok_dev * blocks, dtype=jnp.int32)[None, :]
    ).astype(jnp.bfloat16)
    tok_pieces = tokens.reshape(tok_dev * blocks, piece)
    og_pieces = out_grad.reshape(tok_dev * blocks, piece)
    send_x = jnp.dot(select, tok_pieces, preferred_element_type=jnp.float32).astype(jnp.bfloat16)
    gate_val = jnp.where(valid, gate_flat[safe].astype(jnp.float32) * (1.0 / 65536.0), 0.0)
    gate_rows = jnp.repeat(gate_val, blocks)
    og_sel = jnp.dot(select, og_pieces, preferred_element_type=jnp.float32)
    send_dy = (gate_rows[:, None] * og_sel).astype(jnp.bfloat16)
    x_flat, dy_flat = exchange(send_x, send_dy)
    x_rows = x_flat.reshape(experts * capacity, width)
    dy_rows = dy_flat.reshape(experts * capacity, width)
    down_local, row_grad = expert_math(x_rows, dy_rows, w_gate_e, w_up_e, w_down_e)
    (returned,) = exchange(row_grad.reshape(experts * tile_rows, piece))
    total = jnp.dot(select.T, returned, preferred_element_type=jnp.float32)
    token_grad = total.reshape(tok_dev, width).astype(jnp.bfloat16)
    return (token_grad, down_local[None])


def solution(mesh):
    return jax.shard_map(
        body,
        mesh=mesh,
        in_specs=(
            P(("node", "local"), None),
            P(("node", "local"), None),
            P(("node", "local"), None),
            P(("node", "local"), None),
            P(("node", "local"), None),
            P(("node", "local"), None, None),
            P(("node", "local"), None, None),
            P(("node", "local"), None, None),
        ),
        out_specs=(P(("node", "local"), None), P(("node", "local"), None, None)),
        check_vma=False,
    )
```

```python
import functools
import jax
import jax.numpy as jnp
from jax import lax
from jax.sharding import PartitionSpec as P
from jax.experimental import pallas as pl
from jax.experimental.pallas import tpu as pltpu


def _exchange_kernel(n_local, *refs):
    count = (len(refs) - 2) // 2
    srcs = refs[:count]
    dsts = refs[count:2 * count]
    send_sems = refs[2 * count]
    recv_sems = refs[2 * count + 1]
    node = lax.axis_index("node")
    local = lax.axis_index("local")
    me = node * n_local + local
    devices = lax.axis_size("node") * n_local
    rows = srcs[0].shape[0] // devices

    def copy_to(p, i):
        return pltpu.make_async_remote_copy(
            src_ref=srcs[i].at[pl.ds(p * rows, rows)],
            dst_ref=dsts[i].at[pl.ds(me * rows, rows)],
            send_sem=send_sems.at[i],
            recv_sem=recv_sems.at[i],
            device_id=(p // n_local, p % n_local),
            device_id_type=pl.DeviceIdType.MESH,
        )

    def local_copy(i):
        return pltpu.make_async_copy(
            srcs[i].at[pl.ds(me * rows, rows)],
            dsts[i].at[pl.ds(me * rows, rows)],
            recv_sems.at[i],
        )

    for i in range(count):
        local_copy(i).start()

    core = node % 2
    y_pos = (node // 2) % 4
    z_pos = node // 8

    def start_body(step, carry):
        t = step % 64
        d_core = step // 64
        dx = t % 4
        dy = (t // 4 + dx) % 4
        dz = (t // 16 + t // 4 + dx) % 4
        node_to = (((z_pos + dz) % 4) * 4 + (y_pos + dy) % 4) * 2 + (core + d_core) % 2
        p = node_to * n_local + (local + dx) % 4
        for i in range(count):
            copy_to(p, i).start()
        return carry

    lax.fori_loop(1, devices, start_body, 0)
    nxt = lax.rem(me + 1, devices)
    for i in range(count):
        pltpu.make_async_copy(dsts[i], dsts[i], recv_sems.at[i]).wait()
        pltpu.make_async_remote_copy(
            src_ref=srcs[i].at[pl.ds(0, (devices - 1) * rows)],
            dst_ref=dsts[i].at[pl.ds(0, (devices - 1) * rows)],
            send_sem=send_sems.at[i],
            recv_sem=recv_sems.at[i],
            device_id=(nxt // n_local, nxt % n_local),
            device_id_type=pl.DeviceIdType.MESH,
        ).wait_send()


def exchange(*arrays):
    n_local = lax.axis_size("local")
    count = len(arrays)
    return pl.pallas_call(
        functools.partial(_exchange_kernel, n_local),
        out_shape=[jax.ShapeDtypeStruct(a.shape, a.dtype) for a in arrays],
        in_specs=[pl.BlockSpec(memory_space=pl.ANY)] * count,
        out_specs=[pl.BlockSpec(memory_space=pl.ANY)] * count,
        scratch_shapes=[
            pltpu.SemaphoreType.DMA((count,)),
            pltpu.SemaphoreType.DMA((count,)),
        ],
        compiler_params=pltpu.CompilerParams(has_side_effects=True),
    )(*arrays)


def expert_math(x_rows, dy_rows, w_gate_e, w_up_e, w_down_e):
    gate_act = jnp.dot(x_rows, w_gate_e, preferred_element_type=jnp.float32)
    up_act = jnp.dot(x_rows, w_up_e, preferred_element_type=jnp.float32)
    sig = jax.nn.sigmoid(gate_act)
    hidden = (gate_act * sig * up_act).astype(jnp.bfloat16)
    contract_rows = (((0,), (0,)), ((), ()))
    contract_last = (((1,), (1,)), ((), ()))
    down_local = lax.dot_general(
        hidden, dy_rows, contract_rows, preferred_element_type=jnp.float32
    ).astype(jnp.bfloat16)
    hidden_grad = lax.dot_general(
        dy_rows, w_down_e, contract_last, preferred_element_type=jnp.float32
    )
    gate_grad = (hidden_grad * up_act * sig * (1.0 + gate_act * (1.0 - sig))).astype(jnp.bfloat16)
    up_grad = (hidden_grad * gate_act * sig).astype(jnp.bfloat16)
    row_grad = (
        lax.dot_general(gate_grad, w_gate_e, contract_last, preferred_element_type=jnp.float32)
        + lax.dot_general(up_grad, w_up_e, contract_last, preferred_element_type=jnp.float32)
    ).astype(jnp.bfloat16)
    return (down_local, row_grad)


def body(
    tokens, out_grad, node_lists, expert_local, gate_fixed, gate_weight, up_weight, down_weight
):
    nodes = lax.axis_size("node")
    per_node = lax.axis_size("local")
    experts = nodes * per_node
    tok_dev, top_count = expert_local.shape
    width = tokens.shape[1]
    capacity = tok_dev * top_count // experts
    node_pick = jnp.take_along_axis(node_lists, expert_local // per_node, axis=1)
    expert_ids = (node_pick * per_node + expert_local % per_node).reshape(-1)
    onehot = (expert_ids[:, None] == jnp.arange(experts, dtype=jnp.int32)[None, :]).astype(
        jnp.int32
    )
    running = jnp.cumsum(onehot, axis=0)
    slot = jnp.sum(onehot * running, axis=1) - 1
    kept = slot < capacity
    position = jnp.where(kept, expert_ids * capacity + slot, experts * capacity)
    w_gate_e = gate_weight[0]
    w_up_e = up_weight[0]
    w_down_e = down_weight[0]
    gate_flat = gate_fixed.reshape(-1)
    table = jnp.full((experts * capacity,), -1, jnp.int32)
    table = table.at[position].set(jnp.arange(tok_dev * top_count, dtype=jnp.int32), mode="drop")
    valid = table >= 0
    safe = jnp.maximum(table, 0)
    rows = safe // top_count
    tile_rows = 8
    blocks = tile_rows // capacity
    piece = width // blocks
    slot_token = jnp.where(valid, rows, -1)
    row_key = jnp.where(
        jnp.repeat(valid, blocks),
        jnp.repeat(slot_token, blocks) * blocks + jnp.arange(experts * tile_rows, dtype=jnp.int32) % blocks,
        -1,
    )
    select = (
        row_key[:, None] == jnp.arange(tok_dev * blocks, dtype=jnp.int32)[None, :]
    ).astype(jnp.bfloat16)
    n_sel = tok_dev * blocks
    sources = jnp.concatenate(
        [tokens.reshape(n_sel, piece), out_grad.reshape(n_sel, piece)], axis=0
    )
    select2 = jnp.concatenate(
        [
            jnp.concatenate([select.reshape(experts, tile_rows, n_sel), jnp.zeros((experts, tile_rows, n_sel), jnp.bfloat16)], axis=2),
            jnp.concatenate([jnp.zeros((experts, tile_rows, n_sel), jnp.bfloat16), select.reshape(experts, tile_rows, n_sel)], axis=2),
        ],
        axis=1,
    ).reshape(experts * 2 * tile_rows, 2 * n_sel)
    gate_val = jnp.where(valid, gate_flat[safe].astype(jnp.float32) * (1.0 / 65536.0), 0.0)
    scale = jnp.concatenate(
        [jnp.ones((experts, tile_rows), jnp.float32), jnp.repeat(gate_val, blocks).reshape(experts, tile_rows)],
        axis=1,
    ).reshape(-1)
    picked = jnp.dot(select2, sources, preferred_element_type=jnp.float32)
    send_both = (scale[:, None] * picked).astype(jnp.bfloat16)
    (recv_both,) = exchange(send_both)
    recv_both = recv_both.reshape(experts, 2 * tile_rows, piece)
    x_rows = recv_both[:, :tile_rows].reshape(experts * capacity, width)
    dy_rows = recv_both[:, tile_rows:].reshape(experts * capacity, width)
    down_local, row_grad = expert_math(x_rows, dy_rows, w_gate_e, w_up_e, w_down_e)
    (returned,) = exchange(row_grad.reshape(experts * tile_rows, piece))
    total = jnp.dot(select.T, returned, preferred_element_type=jnp.float32)
    token_grad = total.reshape(tok_dev, width).astype(jnp.bfloat16)
    return (token_grad, down_local[None])


def solution(mesh):
    return jax.shard_map(
        body,
        mesh=mesh,
        in_specs=(
            P(("node", "local"), None),
            P(("node", "local"), None),
            P(("node", "local"), None),
            P(("node", "local"), None),
            P(("node", "local"), None),
            P(("node", "local"), None, None),
            P(("node", "local"), None, None),
            P(("node", "local"), None, None),
        ),
        out_specs=(P(("node", "local"), None), P(("node", "local"), None, None)),
        check_vma=False,
    )
```

```python
import functools
import jax
import jax.numpy as jnp
from jax import lax
from jax.sharding import PartitionSpec as P
from jax.experimental import pallas as pl
from jax.experimental.pallas import tpu as pltpu


def _exchange_kernel(n_local, count, n_work_in, n_work_out, work, *refs):
    srcs = refs[:count]
    work_in = refs[count:count + n_work_in]
    base = count + n_work_in
    dsts = refs[base:base + count]
    work_out = refs[base + count:base + count + n_work_out]
    base = base + count + n_work_out
    send_sems = refs[base]
    recv_sems = refs[base + 1]
    work_scratch = refs[base + 2:]
    node = lax.axis_index("node")
    local = lax.axis_index("local")
    me = node * n_local + local
    devices = lax.axis_size("node") * n_local
    rows = srcs[0].shape[0] // devices

    def copy_to(p, i):
        return pltpu.make_async_remote_copy(
            src_ref=srcs[i].at[pl.ds(p * rows, rows)],
            dst_ref=dsts[i].at[pl.ds(me * rows, rows)],
            send_sem=send_sems.at[i],
            recv_sem=recv_sems.at[i],
            device_id=(p // n_local, p % n_local),
            device_id_type=pl.DeviceIdType.MESH,
        )

    def local_copy(i):
        return pltpu.make_async_copy(
            srcs[i].at[pl.ds(me * rows, rows)],
            dsts[i].at[pl.ds(me * rows, rows)],
            recv_sems.at[i],
        )

    for i in range(count):
        local_copy(i).start()

    core = node % 2
    y_pos = (node // 2) % 4
    z_pos = node // 8

    def start_body(step, carry):
        t = step % 64
        d_core = step // 64
        dx = t % 4
        dy = (t // 4 + dx) % 4
        dz = (t // 16 + t // 4 + dx) % 4
        node_to = (((z_pos + dz) % 4) * 4 + (y_pos + dy) % 4) * 2 + (core + d_core) % 2
        p = node_to * n_local + (local + dx) % 4
        for i in range(count):
            copy_to(p, i).start()
        return carry

    lax.fori_loop(1, devices, start_body, 0)
    if work is not None:
        work(*work_in, *work_out, *work_scratch)
    nxt = lax.rem(me + 1, devices)
    for i in range(count):
        pltpu.make_async_copy(dsts[i], dsts[i], recv_sems.at[i]).wait()
        pltpu.make_async_remote_copy(
            src_ref=srcs[i].at[pl.ds(0, (devices - 1) * rows)],
            dst_ref=dsts[i].at[pl.ds(0, (devices - 1) * rows)],
            send_sem=send_sems.at[i],
            recv_sem=recv_sems.at[i],
            device_id=(nxt // n_local, nxt % n_local),
            device_id_type=pl.DeviceIdType.MESH,
        ).wait_send()


def exchange(arrays, work=None, work_in=(), work_in_specs=(), work_out=(), work_out_specs=(),
             work_scratch=()):
    n_local = lax.axis_size("local")
    count = len(arrays)
    return pl.pallas_call(
        functools.partial(_exchange_kernel, n_local, count, len(work_in), len(work_out), work),
        out_shape=[jax.ShapeDtypeStruct(a.shape, a.dtype) for a in arrays] + list(work_out),
        in_specs=[pl.BlockSpec(memory_space=pl.ANY)] * count + list(work_in_specs),
        out_specs=[pl.BlockSpec(memory_space=pl.ANY)] * count + list(work_out_specs),
        scratch_shapes=[
            pltpu.SemaphoreType.DMA((count,)),
            pltpu.SemaphoreType.DMA((count,)),
        ] + list(work_scratch),
        compiler_params=pltpu.CompilerParams(has_side_effects=True),
    )(*arrays, *work_in)


def _gate_up_work(x_ref, wg_hbm, wu_hbm, gate_out, up_out, wbuf, wsem):
    k_total = x_ref.shape[1]
    k_step = 512
    copies = [
        pltpu.make_async_copy(w, wbuf.at[i], wsem.at[i]) for i, w in enumerate((wg_hbm, wu_hbm))
    ]
    for c in copies:
        c.start()
    for i, out in enumerate((gate_out, up_out)):
        copies[i].wait()
        out[...] = jnp.zeros(out.shape, out.dtype)

        def step(k, carry, i=i, out=out):
            kk = pl.multiple_of(k * k_step, k_step)
            out[...] += jnp.dot(
                x_ref[:, pl.ds(kk, k_step)], wbuf[i, pl.ds(kk, k_step), :],
                preferred_element_type=jnp.float32,
            )
            return carry

        lax.fori_loop(0, k_total // k_step, step, 0)


def expert_rest(gate_act, up_act, dy_rows, w_gate_e, w_up_e, w_down_e):
    sig = jax.nn.sigmoid(gate_act)
    hidden = (gate_act * sig * up_act).astype(jnp.bfloat16)
    contract_rows = (((0,), (0,)), ((), ()))
    contract_last = (((1,), (1,)), ((), ()))
    down_local = lax.dot_general(
        hidden, dy_rows, contract_rows, preferred_element_type=jnp.float32
    ).astype(jnp.bfloat16)
    hidden_grad = lax.dot_general(
        dy_rows, w_down_e, contract_last, preferred_element_type=jnp.float32
    )
    gate_grad = (hidden_grad * up_act * sig * (1.0 + gate_act * (1.0 - sig))).astype(jnp.bfloat16)
    up_grad = (hidden_grad * gate_act * sig).astype(jnp.bfloat16)
    row_grad = (
        lax.dot_general(gate_grad, w_gate_e, contract_last, preferred_element_type=jnp.float32)
        + lax.dot_general(up_grad, w_up_e, contract_last, preferred_element_type=jnp.float32)
    ).astype(jnp.bfloat16)
    return (down_local, row_grad)


def body(
    tokens, out_grad, node_lists, expert_local, gate_fixed, gate_weight, up_weight, down_weight
):
    nodes = lax.axis_size("node")
    per_node = lax.axis_size("local")
    experts = nodes * per_node
    tok_dev, top_count = expert_local.shape
    width = tokens.shape[1]
    capacity = tok_dev * top_count // experts
    node_pick = jnp.take_along_axis(node_lists, expert_local // per_node, axis=1)
    expert_ids = (node_pick * per_node + expert_local % per_node).reshape(-1)
    onehot = (expert_ids[:, None] == jnp.arange(experts, dtype=jnp.int32)[None, :]).astype(
        jnp.int32
    )
    running = jnp.cumsum(onehot, axis=0)
    slot = jnp.sum(onehot * running, axis=1) - 1
    kept = slot < capacity
    position = jnp.where(kept, expert_ids * capacity + slot, experts * capacity)
    w_gate_e = gate_weight[0]
    w_up_e = up_weight[0]
    w_down_e = down_weight[0]
    gate_flat = gate_fixed.reshape(-1)
    table = jnp.full((experts * capacity,), -1, jnp.int32)
    table = table.at[position].set(jnp.arange(tok_dev * top_count, dtype=jnp.int32), mode="drop")
    valid = table >= 0
    safe = jnp.maximum(table, 0)
    rows = safe // top_count
    tile_rows = 8
    blocks = tile_rows // capacity
    piece = width // blocks
    slot_token = jnp.where(valid, rows, -1)
    row_key = jnp.where(
        jnp.repeat(valid, blocks),
        jnp.repeat(slot_token, blocks) * blocks + jnp.arange(experts * tile_rows, dtype=jnp.int32) % blocks,
        -1,
    )
    select = (
        row_key[:, None] == jnp.arange(tok_dev * blocks, dtype=jnp.int32)[None, :]
    ).astype(jnp.bfloat16)
    tok_pieces = tokens.reshape(tok_dev * blocks, piece)
    og_pieces = out_grad.reshape(tok_dev * blocks, piece)
    send_x = jnp.dot(select, tok_pieces, preferred_element_type=jnp.float32).astype(jnp.bfloat16)
    gate_val = jnp.where(valid, gate_flat[safe].astype(jnp.float32) * (1.0 / 65536.0), 0.0)
    gate_rows = jnp.repeat(gate_val, blocks)
    og_sel = jnp.dot(select, og_pieces, preferred_element_type=jnp.float32)
    send_dy = (gate_rows[:, None] * og_sel).astype(jnp.bfloat16)
    (x_flat,) = exchange([send_x])
    x_rows = x_flat.reshape(experts * capacity, width)
    hid = w_gate_e.shape[1]
    n_rows = experts * capacity
    dy_flat, gate_act, up_act = exchange(
        [send_dy],
        work=_gate_up_work,
        work_in=(x_rows, w_gate_e, w_up_e),
        work_in_specs=(
            pl.BlockSpec(memory_space=pltpu.VMEM),
            pl.BlockSpec(memory_space=pl.ANY),
            pl.BlockSpec(memory_space=pl.ANY),
        ),
        work_out=(
            jax.ShapeDtypeStruct((n_rows, hid), jnp.float32),
            jax.ShapeDtypeStruct((n_rows, hid), jnp.float32),
        ),
        work_out_specs=(pl.BlockSpec(memory_space=pltpu.VMEM),) * 2,
        work_scratch=(
            pltpu.VMEM((2,) + w_gate_e.shape, w_gate_e.dtype),
            pltpu.SemaphoreType.DMA((2,)),
        ),
    )
    dy_rows = dy_flat.reshape(experts * capacity, width)
    down_local, row_grad = expert_rest(gate_act, up_act, dy_rows, w_gate_e, w_up_e, w_down_e)
    (returned,) = exchange([row_grad.reshape(experts * tile_rows, piece)])
    total = jnp.dot(select.T, returned, preferred_element_type=jnp.float32)
    token_grad = total.reshape(tok_dev, width).astype(jnp.bfloat16)
    return (token_grad, down_local[None])


def solution(mesh):
    return jax.shard_map(
        body,
        mesh=mesh,
        in_specs=(
            P(("node", "local"), None),
            P(("node", "local"), None),
            P(("node", "local"), None),
            P(("node", "local"), None),
            P(("node", "local"), None),
            P(("node", "local"), None, None),
            P(("node", "local"), None, None),
            P(("node", "local"), None, None),
        ),
        out_specs=(P(("node", "local"), None), P(("node", "local"), None, None)),
        check_vma=False,
    )
```

```python
import functools
import jax
import jax.numpy as jnp
from jax import lax
from jax.sharding import PartitionSpec as P
from jax.experimental import pallas as pl
from jax.experimental.pallas import tpu as pltpu


def _exchange_kernel(n_local, count, n_work_in, n_work_out, work, *refs):
    srcs = refs[:count]
    work_in = refs[count:count + n_work_in]
    base = count + n_work_in
    dsts = refs[base:base + count]
    work_out = refs[base + count:base + count + n_work_out]
    base = base + count + n_work_out
    send_sems = refs[base]
    recv_sems = refs[base + 1]
    work_scratch = refs[base + 2:]
    node = lax.axis_index("node")
    local = lax.axis_index("local")
    me = node * n_local + local
    devices = lax.axis_size("node") * n_local
    rows = srcs[0].shape[0] // devices

    def copy_to(p, i):
        return pltpu.make_async_remote_copy(
            src_ref=srcs[i].at[pl.ds(p * rows, rows)],
            dst_ref=dsts[i].at[pl.ds(me * rows, rows)],
            send_sem=send_sems.at[i],
            recv_sem=recv_sems.at[i],
            device_id=(p // n_local, p % n_local),
            device_id_type=pl.DeviceIdType.MESH,
        )

    def local_copy(i):
        return pltpu.make_async_copy(
            srcs[i].at[pl.ds(me * rows, rows)],
            dsts[i].at[pl.ds(me * rows, rows)],
            recv_sems.at[i],
        )

    for i in range(count):
        local_copy(i).start()

    core = node % 2
    y_pos = (node // 2) % 4
    z_pos = node // 8

    def start_body(step, carry):
        t = step % 64
        d_core = step // 64
        dx = t % 4
        dy = (t // 4 + dx) % 4
        dz = (t // 16 + t // 4 + dx) % 4
        node_to = (((z_pos + dz) % 4) * 4 + (y_pos + dy) % 4) * 2 + (core + d_core) % 2
        p = node_to * n_local + (local + dx) % 4
        for i in range(count):
            copy_to(p, i).start()
        return carry

    lax.fori_loop(1, devices, start_body, 0)
    if work is not None:
        work(*work_in, *work_out, *work_scratch)
    nxt = lax.rem(me + 1, devices)
    for i in range(count):
        pltpu.make_async_copy(dsts[i], dsts[i], recv_sems.at[i]).wait()
        pltpu.make_async_remote_copy(
            src_ref=srcs[i].at[pl.ds(0, (devices - 1) * rows)],
            dst_ref=dsts[i].at[pl.ds(0, (devices - 1) * rows)],
            send_sem=send_sems.at[i],
            recv_sem=recv_sems.at[i],
            device_id=(nxt // n_local, nxt % n_local),
            device_id_type=pl.DeviceIdType.MESH,
        ).wait_send()


def exchange(arrays, work=None, work_in=(), work_in_specs=(), work_out=(), work_out_specs=(),
             work_scratch=()):
    n_local = lax.axis_size("local")
    count = len(arrays)
    return pl.pallas_call(
        functools.partial(_exchange_kernel, n_local, count, len(work_in), len(work_out), work),
        out_shape=[jax.ShapeDtypeStruct(a.shape, a.dtype) for a in arrays] + list(work_out),
        in_specs=[pl.BlockSpec(memory_space=pl.ANY)] * count + list(work_in_specs),
        out_specs=[pl.BlockSpec(memory_space=pl.ANY)] * count + list(work_out_specs),
        scratch_shapes=[
            pltpu.SemaphoreType.DMA((count,)),
            pltpu.SemaphoreType.DMA((count,)),
        ] + list(work_scratch),
        compiler_params=pltpu.CompilerParams(has_side_effects=True),
    )(*arrays, *work_in)


def _down_grad_work(hidden_t_ref, dy_ref, down_out):
    n_step = 512

    def step(c, carry):
        cc = pl.multiple_of(c * n_step, n_step)
        down_out[:, pl.ds(cc, n_step)] = jnp.dot(
            hidden_t_ref[...], dy_ref[:, pl.ds(cc, n_step)], preferred_element_type=jnp.float32
        ).astype(down_out.dtype)
        return carry

    lax.fori_loop(0, dy_ref.shape[1] // n_step, step, 0)


def expert_math(x_rows, dy_rows, w_gate_e, w_up_e, w_down_e):
    gate_act = jnp.dot(x_rows, w_gate_e, preferred_element_type=jnp.float32)
    up_act = jnp.dot(x_rows, w_up_e, preferred_element_type=jnp.float32)
    sig = jax.nn.sigmoid(gate_act)
    hidden = (gate_act * sig * up_act).astype(jnp.bfloat16)
    contract_rows = (((0,), (0,)), ((), ()))
    contract_last = (((1,), (1,)), ((), ()))
    hidden_grad = lax.dot_general(
        dy_rows, w_down_e, contract_last, preferred_element_type=jnp.float32
    )
    gate_grad = (hidden_grad * up_act * sig * (1.0 + gate_act * (1.0 - sig))).astype(jnp.bfloat16)
    up_grad = (hidden_grad * gate_act * sig).astype(jnp.bfloat16)
    row_grad = (
        lax.dot_general(gate_grad, w_gate_e, contract_last, preferred_element_type=jnp.float32)
        + lax.dot_general(up_grad, w_up_e, contract_last, preferred_element_type=jnp.float32)
    ).astype(jnp.bfloat16)
    return (hidden, row_grad)


def body(
    tokens, out_grad, node_lists, expert_local, gate_fixed, gate_weight, up_weight, down_weight
):
    nodes = lax.axis_size("node")
    per_node = lax.axis_size("local")
    experts = nodes * per_node
    tok_dev, top_count = expert_local.shape
    width = tokens.shape[1]
    capacity = tok_dev * top_count // experts
    node_pick = jnp.take_along_axis(node_lists, expert_local // per_node, axis=1)
    expert_ids = (node_pick * per_node + expert_local % per_node).reshape(-1)
    onehot = (expert_ids[:, None] == jnp.arange(experts, dtype=jnp.int32)[None, :]).astype(
        jnp.int32
    )
    running = jnp.cumsum(onehot, axis=0)
    slot = jnp.sum(onehot * running, axis=1) - 1
    kept = slot < capacity
    position = jnp.where(kept, expert_ids * capacity + slot, experts * capacity)
    w_gate_e = gate_weight[0]
    w_up_e = up_weight[0]
    w_down_e = down_weight[0]
    gate_flat = gate_fixed.reshape(-1)
    table = jnp.full((experts * capacity,), -1, jnp.int32)
    table = table.at[position].set(jnp.arange(tok_dev * top_count, dtype=jnp.int32), mode="drop")
    valid = table >= 0
    safe = jnp.maximum(table, 0)
    rows = safe // top_count
    tile_rows = 8
    blocks = tile_rows // capacity
    piece = width // blocks
    slot_token = jnp.where(valid, rows, -1)
    row_key = jnp.where(
        jnp.repeat(valid, blocks),
        jnp.repeat(slot_token, blocks) * blocks + jnp.arange(experts * tile_rows, dtype=jnp.int32) % blocks,
        -1,
    )
    select = (
        row_key[:, None] == jnp.arange(tok_dev * blocks, dtype=jnp.int32)[None, :]
    ).astype(jnp.bfloat16)
    tok_pieces = tokens.reshape(tok_dev * blocks, piece)
    og_pieces = out_grad.reshape(tok_dev * blocks, piece)
    send_x = jnp.dot(select, tok_pieces, preferred_element_type=jnp.float32).astype(jnp.bfloat16)
    gate_val = jnp.where(valid, gate_flat[safe].astype(jnp.float32) * (1.0 / 65536.0), 0.0)
    gate_rows = jnp.repeat(gate_val, blocks)
    og_sel = jnp.dot(select, og_pieces, preferred_element_type=jnp.float32)
    send_dy = (gate_rows[:, None] * og_sel).astype(jnp.bfloat16)
    x_flat, dy_flat = exchange([send_x, send_dy])
    x_rows = x_flat.reshape(experts * capacity, width)
    dy_rows = dy_flat.reshape(experts * capacity, width)
    hidden, row_grad = expert_math(x_rows, dy_rows, w_gate_e, w_up_e, w_down_e)
    returned, down_local = exchange(
        [row_grad.reshape(experts * tile_rows, piece)],
        work=_down_grad_work,
        work_in=(hidden.T, dy_rows),
        work_in_specs=(pl.BlockSpec(memory_space=pltpu.VMEM),) * 2,
        work_out=(jax.ShapeDtypeStruct((hidden.shape[1], width), jnp.bfloat16),),
        work_out_specs=(pl.BlockSpec(memory_space=pltpu.VMEM),),
    )
    total = jnp.dot(select.T, returned, preferred_element_type=jnp.float32)
    token_grad = total.reshape(tok_dev, width).astype(jnp.bfloat16)
    return (token_grad, down_local[None])


def solution(mesh):
    return jax.shard_map(
        body,
        mesh=mesh,
        in_specs=(
            P(("node", "local"), None),
            P(("node", "local"), None),
            P(("node", "local"), None),
            P(("node", "local"), None),
            P(("node", "local"), None),
            P(("node", "local"), None, None),
            P(("node", "local"), None, None),
            P(("node", "local"), None, None),
        ),
        out_specs=(P(("node", "local"), None), P(("node", "local"), None, None)),
        check_vma=False,
    )
```

```python
import functools
import jax
import jax.numpy as jnp
from jax import lax
from jax.sharding import PartitionSpec as P
from jax.experimental import pallas as pl
from jax.experimental.pallas import tpu as pltpu


def _exchange_kernel(n_local, *refs):
    count = (len(refs) - 2) // 2
    srcs = refs[:count]
    dsts = refs[count:2 * count]
    send_sems = refs[2 * count]
    recv_sems = refs[2 * count + 1]
    node = lax.axis_index("node")
    local = lax.axis_index("local")
    me = node * n_local + local
    devices = lax.axis_size("node") * n_local
    rows = srcs[0].shape[0] // devices

    def copy_to(p, i):
        return pltpu.make_async_remote_copy(
            src_ref=srcs[i].at[pl.ds(p * rows, rows)],
            dst_ref=dsts[i].at[pl.ds(me * rows, rows)],
            send_sem=send_sems.at[i],
            recv_sem=recv_sems.at[i],
            device_id=(p // n_local, p % n_local),
            device_id_type=pl.DeviceIdType.MESH,
        )

    def local_copy(i):
        return pltpu.make_async_copy(
            srcs[i].at[pl.ds(me * rows, rows)],
            dsts[i].at[pl.ds(me * rows, rows)],
            recv_sems.at[i],
        )

    for i in range(count):
        local_copy(i).start()

    core = node % 2
    y_pos = (node // 2) % 4
    z_pos = node // 8

    def start_body(step, carry):
        t = step % 64
        d_core = step // 64
        dx = t % 4
        dy = (t // 4 + dx) % 4
        dz = (t // 16 + t // 4 + dx) % 4
        node_to = (((z_pos + dz) % 4) * 4 + (y_pos + dy) % 4) * 2 + (core + d_core) % 2
        p = node_to * n_local + (local + dx) % 4
        for i in range(count):
            copy_to(p, i).start()
        return carry

    lax.fori_loop(1, devices, start_body, 0)
    nxt = lax.rem(me + 1, devices)
    for i in range(count):
        pltpu.make_async_copy(dsts[i], dsts[i], recv_sems.at[i]).wait()
        pltpu.make_async_remote_copy(
            src_ref=srcs[i].at[pl.ds(0, (devices - 1) * rows)],
            dst_ref=dsts[i].at[pl.ds(0, (devices - 1) * rows)],
            send_sem=send_sems.at[i],
            recv_sem=recv_sems.at[i],
            device_id=(nxt // n_local, nxt % n_local),
            device_id_type=pl.DeviceIdType.MESH,
        ).wait_send()


def exchange(*arrays):
    n_local = lax.axis_size("local")
    count = len(arrays)
    return pl.pallas_call(
        functools.partial(_exchange_kernel, n_local),
        out_shape=[jax.ShapeDtypeStruct(a.shape, a.dtype) for a in arrays],
        in_specs=[pl.BlockSpec(memory_space=pl.ANY)] * count,
        out_specs=[pl.BlockSpec(memory_space=pl.ANY)] * count,
        scratch_shapes=[
            pltpu.SemaphoreType.DMA((count,)),
            pltpu.SemaphoreType.DMA((count,)),
        ],
        compiler_params=pltpu.CompilerParams(has_side_effects=True),
    )(*arrays)


def _expert_kernel(x_ref, dy_ref, wg_hbm, wu_hbm, wd_hbm, row_out, down_hbm,
                   wg, wu, wd, gate_act, up_act, hidden_grad, down_buf, wsem, osem):
    k_total = x_ref.shape[1]
    step = 512
    n_steps = k_total // step
    nt = (((1,), (1,)), ((), ()))
    loads = [
        pltpu.make_async_copy(src, dst, wsem.at[i])
        for i, (src, dst) in enumerate(((wg_hbm, wg), (wu_hbm, wu), (wd_hbm, wd)))
    ]
    for c in loads:
        c.start()

    def project(w, out):
        out[...] = jnp.zeros(out.shape, out.dtype)

        def body(k, carry):
            kk = pl.multiple_of(k * step, step)
            out[...] += jnp.dot(
                x_ref[:, pl.ds(kk, step)], w[pl.ds(kk, step), :], preferred_element_type=jnp.float32
            )
            return carry

        lax.fori_loop(0, n_steps, body, 0)

    loads[0].wait()
    project(wg, gate_act)
    loads[1].wait()
    project(wu, up_act)
    loads[2].wait()
    hidden_grad[...] = jnp.zeros(hidden_grad.shape, hidden_grad.dtype)

    def hg_body(k, carry):
        kk = pl.multiple_of(k * step, step)
        hidden_grad[...] += lax.dot_general(
            dy_ref[:, pl.ds(kk, step)], wd[:, pl.ds(kk, step)], nt,
            preferred_element_type=jnp.float32,
        )
        return carry

    lax.fori_loop(0, n_steps, hg_body, 0)
    g = gate_act[...]
    u = up_act[...]
    hg = hidden_grad[...]
    sig = 1.0 / (1.0 + jnp.exp(-g))
    hidden = (g * sig * u).astype(jnp.bfloat16)
    gate_grad = (hg * u * sig * (1.0 + g * (1.0 - sig))).astype(jnp.bfloat16)
    up_grad = (hg * g * sig).astype(jnp.bfloat16)
    hidden_t = jnp.transpose(hidden.astype(jnp.float32)).astype(jnp.bfloat16)

    def out_body(c, carry):
        cc = pl.multiple_of(c * step, step)
        row_out[:, pl.ds(cc, step)] = (
            lax.dot_general(gate_grad, wg[pl.ds(cc, step), :], nt, preferred_element_type=jnp.float32)
            + lax.dot_general(up_grad, wu[pl.ds(cc, step), :], nt, preferred_element_type=jnp.float32)
        ).astype(row_out.dtype)
        slot = c % 2

        @pl.when(c >= 2)
        def _():
            pltpu.make_async_copy(
                down_buf.at[slot], down_hbm.at[:, pl.ds(cc - 2 * step, step)], osem.at[slot]
            ).wait()

        down_buf[slot] = jnp.dot(
            hidden_t, dy_ref[:, pl.ds(cc, step)], preferred_element_type=jnp.float32
        ).astype(down_buf.dtype)
        pltpu.make_async_copy(down_buf.at[slot], down_hbm.at[:, pl.ds(cc, step)], osem.at[slot]).start()
        return carry

    lax.fori_loop(0, n_steps, out_body, 0)
    for c in (n_steps - 2, n_steps - 1):
        pltpu.make_async_copy(
            down_buf.at[c % 2], down_hbm.at[:, pl.ds(c * step, step)], osem.at[c % 2]
        ).wait()


def expert_math(x_rows, dy_rows, w_gate_e, w_up_e, w_down_e):
    n_rows, width = x_rows.shape
    hid = w_gate_e.shape[1]
    vmem = pl.BlockSpec(memory_space=pltpu.VMEM)
    hbm = pl.BlockSpec(memory_space=pl.ANY)
    row_grad, down_local = pl.pallas_call(
        _expert_kernel,
        out_shape=[
            jax.ShapeDtypeStruct((n_rows, width), jnp.bfloat16),
            jax.ShapeDtypeStruct((hid, width), jnp.bfloat16),
        ],
        in_specs=[vmem, vmem, hbm, hbm, hbm],
        out_specs=[vmem, hbm],
        scratch_shapes=[
            pltpu.VMEM(w_gate_e.shape, w_gate_e.dtype),
            pltpu.VMEM(w_up_e.shape, w_up_e.dtype),
            pltpu.VMEM(w_down_e.shape, w_down_e.dtype),
            pltpu.VMEM((n_rows, hid), jnp.float32),
            pltpu.VMEM((n_rows, hid), jnp.float32),
            pltpu.VMEM((n_rows, hid), jnp.float32),
            pltpu.VMEM((2, hid, 512), jnp.bfloat16),
            pltpu.SemaphoreType.DMA((3,)),
            pltpu.SemaphoreType.DMA((2,)),
        ],
        compiler_params=pltpu.CompilerParams(vmem_limit_bytes=60 * 1024 * 1024),
    )(x_rows, dy_rows, w_gate_e, w_up_e, w_down_e)
    return (down_local, row_grad)


def body(
    tokens, out_grad, node_lists, expert_local, gate_fixed, gate_weight, up_weight, down_weight
):
    nodes = lax.axis_size("node")
    per_node = lax.axis_size("local")
    experts = nodes * per_node
    tok_dev, top_count = expert_local.shape
    width = tokens.shape[1]
    capacity = tok_dev * top_count // experts
    node_pick = jnp.take_along_axis(node_lists, expert_local // per_node, axis=1)
    expert_ids = (node_pick * per_node + expert_local % per_node).reshape(-1)
    onehot = (expert_ids[:, None] == jnp.arange(experts, dtype=jnp.int32)[None, :]).astype(
        jnp.int32
    )
    running = jnp.cumsum(onehot, axis=0)
    slot = jnp.sum(onehot * running, axis=1) - 1
    kept = slot < capacity
    position = jnp.where(kept, expert_ids * capacity + slot, experts * capacity)
    w_gate_e = gate_weight[0]
    w_up_e = up_weight[0]
    w_down_e = down_weight[0]
    gate_flat = gate_fixed.reshape(-1)
    table = jnp.full((experts * capacity,), -1, jnp.int32)
    table = table.at[position].set(jnp.arange(tok_dev * top_count, dtype=jnp.int32), mode="drop")
    valid = table >= 0
    safe = jnp.maximum(table, 0)
    rows = safe // top_count
    tile_rows = 8
    blocks = tile_rows // capacity
    piece = width // blocks
    slot_token = jnp.where(valid, rows, -1)
    row_key = jnp.where(
        jnp.repeat(valid, blocks),
        jnp.repeat(slot_token, blocks) * blocks + jnp.arange(experts * tile_rows, dtype=jnp.int32) % blocks,
        -1,
    )
    select = (
        row_key[:, None] == jnp.arange(tok_dev * blocks, dtype=jnp.int32)[None, :]
    ).astype(jnp.bfloat16)
    tok_pieces = tokens.reshape(tok_dev * blocks, piece)
    og_pieces = out_grad.reshape(tok_dev * blocks, piece)
    send_x = jnp.dot(select, tok_pieces, preferred_element_type=jnp.float32).astype(jnp.bfloat16)
    gate_val = jnp.where(valid, gate_flat[safe].astype(jnp.float32) * (1.0 / 65536.0), 0.0)
    gate_rows = jnp.repeat(gate_val, blocks)
    og_sel = jnp.dot(select, og_pieces, preferred_element_type=jnp.float32)
    send_dy = (gate_rows[:, None] * og_sel).astype(jnp.bfloat16)
    x_flat, dy_flat = exchange(send_x, send_dy)
    x_rows = x_flat.reshape(experts * capacity, width)
    dy_rows = dy_flat.reshape(experts * capacity, width)
    down_local, row_grad = expert_math(x_rows, dy_rows, w_gate_e, w_up_e, w_down_e)
    (returned,) = exchange(row_grad.reshape(experts * tile_rows, piece))
    total = jnp.dot(select.T, returned, preferred_element_type=jnp.float32)
    token_grad = total.reshape(tok_dev, width).astype(jnp.bfloat16)
    return (token_grad, down_local[None])


def solution(mesh):
    return jax.shard_map(
        body,
        mesh=mesh,
        in_specs=(
            P(("node", "local"), None),
            P(("node", "local"), None),
            P(("node", "local"), None),
            P(("node", "local"), None),
            P(("node", "local"), None),
            P(("node", "local"), None, None),
            P(("node", "local"), None, None),
            P(("node", "local"), None, None),
        ),
        out_specs=(P(("node", "local"), None), P(("node", "local"), None, None)),
        check_vma=False,
    )
```

```python
import functools
import jax
import jax.numpy as jnp
from jax import lax
from jax.sharding import PartitionSpec as P
from jax.experimental import pallas as pl
from jax.experimental.pallas import tpu as pltpu


def _exchange_kernel(n_local, *refs):
    count = (len(refs) - 2) // 2
    srcs = refs[:count]
    dsts = refs[count:2 * count]
    send_sems = refs[2 * count]
    recv_sems = refs[2 * count + 1]
    node = lax.axis_index("node")
    local = lax.axis_index("local")
    me = node * n_local + local
    devices = lax.axis_size("node") * n_local
    rows = srcs[0].shape[0] // devices

    def copy_to(p, i):
        return pltpu.make_async_remote_copy(
            src_ref=srcs[i].at[pl.ds(p * rows, rows)],
            dst_ref=dsts[i].at[pl.ds(me * rows, rows)],
            send_sem=send_sems.at[i],
            recv_sem=recv_sems.at[i],
            device_id=(p // n_local, p % n_local),
            device_id_type=pl.DeviceIdType.MESH,
        )

    def local_copy(i):
        return pltpu.make_async_copy(
            srcs[i].at[pl.ds(me * rows, rows)],
            dsts[i].at[pl.ds(me * rows, rows)],
            recv_sems.at[i],
        )

    for i in range(count):
        local_copy(i).start()

    core = node % 2
    y_pos = (node // 2) % 4
    z_pos = node // 8

    def start_body(step, carry):
        t = step % 64
        d_core = step // 64
        dx = t % 4
        dy = (t // 4 + dx) % 4
        dz = (t // 16 + t // 4 + dx) % 4
        node_to = (((z_pos + dz) % 4) * 4 + (y_pos + dy) % 4) * 2 + (core + d_core) % 2
        p = node_to * n_local + (local + dx) % 4
        for i in range(count):
            copy_to(p, i).start()
        return carry

    lax.fori_loop(1, devices, start_body, 0)
    nxt = lax.rem(me + 1, devices)
    for i in range(count):
        pltpu.make_async_copy(dsts[i], dsts[i], recv_sems.at[i]).wait()
        pltpu.make_async_remote_copy(
            src_ref=srcs[i].at[pl.ds(0, (devices - 1) * rows)],
            dst_ref=dsts[i].at[pl.ds(0, (devices - 1) * rows)],
            send_sem=send_sems.at[i],
            recv_sem=recv_sems.at[i],
            device_id=(nxt // n_local, nxt % n_local),
            device_id_type=pl.DeviceIdType.MESH,
        ).wait_send()


def exchange(*arrays):
    n_local = lax.axis_size("local")
    count = len(arrays)
    return pl.pallas_call(
        functools.partial(_exchange_kernel, n_local),
        out_shape=[jax.ShapeDtypeStruct(a.shape, a.dtype) for a in arrays],
        in_specs=[pl.BlockSpec(memory_space=pl.ANY)] * count,
        out_specs=[pl.BlockSpec(memory_space=pl.ANY)] * count,
        scratch_shapes=[
            pltpu.SemaphoreType.DMA((count,)),
            pltpu.SemaphoreType.DMA((count,)),
        ],
        compiler_params=pltpu.CompilerParams(has_side_effects=True),
    )(*arrays)


def _expert_kernel(x_ref, dy_ref, wg_hbm, wu_hbm, wd_hbm, row_out, down_hbm,
                   wg, wu, wd, gate_act, up_act, hidden_grad, down_buf, wsem, osem):
    k_total = x_ref.shape[1]
    step = 512
    n_steps = k_total // step
    nt = (((1,), (1,)), ((), ()))
    sources = ((wg_hbm, wg), (wu_hbm, wu))

    def row_chunk(i, k):
        src, dst = sources[i]
        kk = pl.multiple_of(k * step, step)
        return pltpu.make_async_copy(src.at[pl.ds(kk, step)], dst.at[pl.ds(kk, step)], wsem.at[i, k])

    def col_chunk(k):
        kk = pl.multiple_of(k * step, step)
        return pltpu.make_async_copy(wd_hbm.at[:, pl.ds(kk, step)], wd.at[:, pl.ds(kk, step)], wsem.at[2, k])

    def start_body(k, carry):
        row_chunk(0, k).start()
        row_chunk(1, k).start()
        return carry

    lax.fori_loop(0, n_steps, start_body, 0)

    def start_wd(k, carry):
        col_chunk(k).start()
        return carry

    lax.fori_loop(0, n_steps, start_wd, 0)
    gate_act[...] = jnp.zeros(gate_act.shape, gate_act.dtype)
    up_act[...] = jnp.zeros(up_act.shape, up_act.dtype)

    def proj_body(k, carry):
        kk = pl.multiple_of(k * step, step)
        x_blk = x_ref[:, pl.ds(kk, step)]
        row_chunk(0, k).wait()
        gate_act[...] += jnp.dot(x_blk, wg[pl.ds(kk, step), :], preferred_element_type=jnp.float32)
        row_chunk(1, k).wait()
        up_act[...] += jnp.dot(x_blk, wu[pl.ds(kk, step), :], preferred_element_type=jnp.float32)
        return carry

    lax.fori_loop(0, n_steps, proj_body, 0)
    hidden_grad[...] = jnp.zeros(hidden_grad.shape, hidden_grad.dtype)

    def hg_body(k, carry):
        kk = pl.multiple_of(k * step, step)
        col_chunk(k).wait()
        hidden_grad[...] += lax.dot_general(
            dy_ref[:, pl.ds(kk, step)], wd[:, pl.ds(kk, step)], nt,
            preferred_element_type=jnp.float32,
        )
        return carry

    lax.fori_loop(0, n_steps, hg_body, 0)
    g = gate_act[...]
    u = up_act[...]
    hg = hidden_grad[...]
    sig = 1.0 / (1.0 + jnp.exp(-g))
    hidden = (g * sig * u).astype(jnp.bfloat16)
    gate_grad = (hg * u * sig * (1.0 + g * (1.0 - sig))).astype(jnp.bfloat16)
    up_grad = (hg * g * sig).astype(jnp.bfloat16)
    hidden_t = jnp.transpose(hidden.astype(jnp.float32)).astype(jnp.bfloat16)

    def out_body(c, carry):
        cc = pl.multiple_of(c * step, step)
        row_out[:, pl.ds(cc, step)] = (
            lax.dot_general(gate_grad, wg[pl.ds(cc, step), :], nt, preferred_element_type=jnp.float32)
            + lax.dot_general(up_grad, wu[pl.ds(cc, step), :], nt, preferred_element_type=jnp.float32)
        ).astype(row_out.dtype)
        slot = c % 2

        @pl.when(c >= 2)
        def _():
            pltpu.make_async_copy(
                down_buf.at[slot], down_hbm.at[:, pl.ds(cc - 2 * step, step)], osem.at[slot]
            ).wait()

        down_buf[slot] = jnp.dot(
            hidden_t, dy_ref[:, pl.ds(cc, step)], preferred_element_type=jnp.float32
        ).astype(down_buf.dtype)
        pltpu.make_async_copy(down_buf.at[slot], down_hbm.at[:, pl.ds(cc, step)], osem.at[slot]).start()
        return carry

    lax.fori_loop(0, n_steps, out_body, 0)
    for c in (n_steps - 2, n_steps - 1):
        pltpu.make_async_copy(
            down_buf.at[c % 2], down_hbm.at[:, pl.ds(c * step, step)], osem.at[c % 2]
        ).wait()


def expert_math(x_rows, dy_rows, w_gate_e, w_up_e, w_down_e):
    n_rows, width = x_rows.shape
    hid = w_gate_e.shape[1]
    vmem = pl.BlockSpec(memory_space=pltpu.VMEM)
    hbm = pl.BlockSpec(memory_space=pl.ANY)
    row_grad, down_local = pl.pallas_call(
        _expert_kernel,
        out_shape=[
            jax.ShapeDtypeStruct((n_rows, width), jnp.bfloat16),
            jax.ShapeDtypeStruct((hid, width), jnp.bfloat16),
        ],
        in_specs=[vmem, vmem, hbm, hbm, hbm],
        out_specs=[vmem, hbm],
        scratch_shapes=[
            pltpu.VMEM(w_gate_e.shape, w_gate_e.dtype),
            pltpu.VMEM(w_up_e.shape, w_up_e.dtype),
            pltpu.VMEM(w_down_e.shape, w_down_e.dtype),
            pltpu.VMEM((n_rows, hid), jnp.float32),
            pltpu.VMEM((n_rows, hid), jnp.float32),
            pltpu.VMEM((n_rows, hid), jnp.float32),
            pltpu.VMEM((2, hid, 512), jnp.bfloat16),
            pltpu.SemaphoreType.DMA((3, width // 512)),
            pltpu.SemaphoreType.DMA((2,)),
        ],
        compiler_params=pltpu.CompilerParams(vmem_limit_bytes=60 * 1024 * 1024),
    )(x_rows, dy_rows, w_gate_e, w_up_e, w_down_e)
    return (down_local, row_grad)


def body(
    tokens, out_grad, node_lists, expert_local, gate_fixed, gate_weight, up_weight, down_weight
):
    nodes = lax.axis_size("node")
    per_node = lax.axis_size("local")
    experts = nodes * per_node
    tok_dev, top_count = expert_local.shape
    width = tokens.shape[1]
    capacity = tok_dev * top_count // experts
    node_pick = jnp.take_along_axis(node_lists, expert_local // per_node, axis=1)
    expert_ids = (node_pick * per_node + expert_local % per_node).reshape(-1)
    onehot = (expert_ids[:, None] == jnp.arange(experts, dtype=jnp.int32)[None, :]).astype(
        jnp.int32
    )
    running = jnp.cumsum(onehot, axis=0)
    slot = jnp.sum(onehot * running, axis=1) - 1
    kept = slot < capacity
    position = jnp.where(kept, expert_ids * capacity + slot, experts * capacity)
    w_gate_e = gate_weight[0]
    w_up_e = up_weight[0]
    w_down_e = down_weight[0]
    gate_flat = gate_fixed.reshape(-1)
    table = jnp.full((experts * capacity,), -1, jnp.int32)
    table = table.at[position].set(jnp.arange(tok_dev * top_count, dtype=jnp.int32), mode="drop")
    valid = table >= 0
    safe = jnp.maximum(table, 0)
    rows = safe // top_count
    tile_rows = 8
    blocks = tile_rows // capacity
    piece = width // blocks
    slot_token = jnp.where(valid, rows, -1)
    row_key = jnp.where(
        jnp.repeat(valid, blocks),
        jnp.repeat(slot_token, blocks) * blocks + jnp.arange(experts * tile_rows, dtype=jnp.int32) % blocks,
        -1,
    )
    select = (
        row_key[:, None] == jnp.arange(tok_dev * blocks, dtype=jnp.int32)[None, :]
    ).astype(jnp.bfloat16)
    tok_pieces = tokens.reshape(tok_dev * blocks, piece)
    og_pieces = out_grad.reshape(tok_dev * blocks, piece)
    send_x = jnp.dot(select, tok_pieces, preferred_element_type=jnp.float32).astype(jnp.bfloat16)
    gate_val = jnp.where(valid, gate_flat[safe].astype(jnp.float32) * (1.0 / 65536.0), 0.0)
    gate_rows = jnp.repeat(gate_val, blocks)
    og_sel = jnp.dot(select, og_pieces, preferred_element_type=jnp.float32)
    send_dy = (gate_rows[:, None] * og_sel).astype(jnp.bfloat16)
    x_flat, dy_flat = exchange(send_x, send_dy)
    x_rows = x_flat.reshape(experts * capacity, width)
    dy_rows = dy_flat.reshape(experts * capacity, width)
    down_local, row_grad = expert_math(x_rows, dy_rows, w_gate_e, w_up_e, w_down_e)
    (returned,) = exchange(row_grad.reshape(experts * tile_rows, piece))
    total = jnp.dot(select.T, returned, preferred_element_type=jnp.float32)
    token_grad = total.reshape(tok_dev, width).astype(jnp.bfloat16)
    return (token_grad, down_local[None])


def solution(mesh):
    return jax.shard_map(
        body,
        mesh=mesh,
        in_specs=(
            P(("node", "local"), None),
            P(("node", "local"), None),
            P(("node", "local"), None),
            P(("node", "local"), None),
            P(("node", "local"), None),
            P(("node", "local"), None, None),
            P(("node", "local"), None, None),
            P(("node", "local"), None, None),
        ),
        out_specs=(P(("node", "local"), None), P(("node", "local"), None, None)),
        check_vma=False,
    )
```

```python
import functools
import jax
import jax.numpy as jnp
from jax import lax
from jax.sharding import PartitionSpec as P
from jax.experimental import pallas as pl
from jax.experimental.pallas import tpu as pltpu


def _exchange_kernel(n_local, *refs):
    count = (len(refs) - 2) // 2
    srcs = refs[:count]
    dsts = refs[count:2 * count]
    send_sems = refs[2 * count]
    recv_sems = refs[2 * count + 1]
    node = lax.axis_index("node")
    local = lax.axis_index("local")
    me = node * n_local + local
    devices = lax.axis_size("node") * n_local
    rows = srcs[0].shape[0] // devices

    def copy_to(p, i):
        return pltpu.make_async_remote_copy(
            src_ref=srcs[i].at[pl.ds(p * rows, rows)],
            dst_ref=dsts[i].at[pl.ds(me * rows, rows)],
            send_sem=send_sems.at[i],
            recv_sem=recv_sems.at[i],
            device_id=(p // n_local, p % n_local),
            device_id_type=pl.DeviceIdType.MESH,
        )

    def local_copy(i):
        return pltpu.make_async_copy(
            srcs[i].at[pl.ds(me * rows, rows)],
            dsts[i].at[pl.ds(me * rows, rows)],
            recv_sems.at[i],
        )

    for i in range(count):
        local_copy(i).start()

    core = node % 2
    y_pos = (node // 2) % 4
    z_pos = node // 8

    def start_body(step, carry):
        t = step % 64
        d_core = step // 64
        dx = t % 4
        dy = (t // 4 + dx) % 4
        dz = (t // 16 + t // 4 + dx) % 4
        node_to = (((z_pos + dz) % 4) * 4 + (y_pos + dy) % 4) * 2 + (core + d_core) % 2
        p = node_to * n_local + (local + dx) % 4
        for i in range(count):
            copy_to(p, i).start()
        return carry

    lax.fori_loop(1, devices, start_body, 0)
    nxt = lax.rem(me + 1, devices)
    for i in range(count):
        pltpu.make_async_copy(dsts[i], dsts[i], recv_sems.at[i]).wait()
        pltpu.make_async_remote_copy(
            src_ref=srcs[i].at[pl.ds(0, (devices - 1) * rows)],
            dst_ref=dsts[i].at[pl.ds(0, (devices - 1) * rows)],
            send_sem=send_sems.at[i],
            recv_sem=recv_sems.at[i],
            device_id=(nxt // n_local, nxt % n_local),
            device_id_type=pl.DeviceIdType.MESH,
        ).wait_send()


def exchange(*arrays):
    n_local = lax.axis_size("local")
    count = len(arrays)
    return pl.pallas_call(
        functools.partial(_exchange_kernel, n_local),
        out_shape=[jax.ShapeDtypeStruct(a.shape, a.dtype) for a in arrays],
        in_specs=[pl.BlockSpec(memory_space=pl.ANY)] * count,
        out_specs=[pl.BlockSpec(memory_space=pl.ANY)] * count,
        scratch_shapes=[
            pltpu.SemaphoreType.DMA((count,)),
            pltpu.SemaphoreType.DMA((count,)),
        ],
        compiler_params=pltpu.CompilerParams(has_side_effects=True),
    )(*arrays)


def _expert_kernel(xf_ref, dyf_ref, wg_hbm, wu_hbm, wd_hbm, row_out, down_hbm,
                   wg, wu, wd, gate_act, up_act, hidden_grad, down_buf, x_ref, dy_ref, wide,
                   wsem, osem):
    k_total = x_ref.shape[1]
    lane = wide.shape[2]
    n_rows = x_ref.shape[0]
    blocks = wide.shape[1] // n_rows
    piece = wide.shape[0] * lane
    for src, dst in ((xf_ref, x_ref), (dyf_ref, dy_ref)):
        for cb in range(wide.shape[0]):
            wide[cb] = src[:, cb * lane:(cb + 1) * lane].astype(jnp.float32)
        for j in range(blocks):
            for cb in range(wide.shape[0]):
                col = j * piece + cb * lane
                dst[:, col:col + lane] = wide[cb, pl.ds(j, n_rows, stride=blocks), :].astype(dst.dtype)
    step = 512
    n_steps = k_total // step
    nt = (((1,), (1,)), ((), ()))
    sources = ((wg_hbm, wg), (wu_hbm, wu))

    def row_chunk(i, k):
        src, dst = sources[i]
        kk = pl.multiple_of(k * step, step)
        return pltpu.make_async_copy(src.at[pl.ds(kk, step)], dst.at[pl.ds(kk, step)], wsem.at[i, k])

    def col_chunk(k):
        kk = pl.multiple_of(k * step, step)
        return pltpu.make_async_copy(wd_hbm.at[:, pl.ds(kk, step)], wd.at[:, pl.ds(kk, step)], wsem.at[2, k])

    def start_body(k, carry):
        row_chunk(0, k).start()
        row_chunk(1, k).start()
        return carry

    lax.fori_loop(0, n_steps, start_body, 0)

    def start_wd(k, carry):
        col_chunk(k).start()
        return carry

    lax.fori_loop(0, n_steps, start_wd, 0)
    gate_act[...] = jnp.zeros(gate_act.shape, gate_act.dtype)
    up_act[...] = jnp.zeros(up_act.shape, up_act.dtype)

    def proj_body(k, carry):
        kk = pl.multiple_of(k * step, step)
        x_blk = x_ref[:, pl.ds(kk, step)]
        row_chunk(0, k).wait()
        gate_act[...] += jnp.dot(x_blk, wg[pl.ds(kk, step), :], preferred_element_type=jnp.float32)
        row_chunk(1, k).wait()
        up_act[...] += jnp.dot(x_blk, wu[pl.ds(kk, step), :], preferred_element_type=jnp.float32)
        return carry

    lax.fori_loop(0, n_steps, proj_body, 0)
    hidden_grad[...] = jnp.zeros(hidden_grad.shape, hidden_grad.dtype)

    def hg_body(k, carry):
        kk = pl.multiple_of(k * step, step)
        col_chunk(k).wait()
        hidden_grad[...] += lax.dot_general(
            dy_ref[:, pl.ds(kk, step)], wd[:, pl.ds(kk, step)], nt,
            preferred_element_type=jnp.float32,
        )
        return carry

    lax.fori_loop(0, n_steps, hg_body, 0)
    g = gate_act[...]
    u = up_act[...]
    hg = hidden_grad[...]
    sig = 1.0 / (1.0 + jnp.exp(-g))
    hidden = (g * sig * u).astype(jnp.bfloat16)
    gate_grad = (hg * u * sig * (1.0 + g * (1.0 - sig))).astype(jnp.bfloat16)
    up_grad = (hg * g * sig).astype(jnp.bfloat16)
    hidden_t = jnp.transpose(hidden.astype(jnp.float32)).astype(jnp.bfloat16)

    for c in range(n_steps):
        cc = c * step
        rg = (
            lax.dot_general(gate_grad, wg[cc:cc + step, :], nt, preferred_element_type=jnp.float32)
            + lax.dot_general(up_grad, wu[cc:cc + step, :], nt, preferred_element_type=jnp.float32)
        ).astype(jnp.bfloat16)
        j, h = divmod(cc, piece)
        for q in range(step // lane):
            wide[h // lane + q, pl.ds(j, n_rows, stride=blocks), :] = (
                rg[:, q * lane:(q + 1) * lane].astype(jnp.float32)
            )
        slot = c % 2
        if c >= 2:
            pltpu.make_async_copy(
                down_buf.at[slot], down_hbm.at[:, cc - 2 * step:cc - step], osem.at[slot]
            ).wait()
        down_buf[slot] = jnp.dot(
            hidden_t, dy_ref[:, cc:cc + step], preferred_element_type=jnp.float32
        ).astype(down_buf.dtype)
        pltpu.make_async_copy(down_buf.at[slot], down_hbm.at[:, cc:cc + step], osem.at[slot]).start()
    for cb in range(wide.shape[0]):
        row_out[:, cb * lane:(cb + 1) * lane] = wide[cb].astype(row_out.dtype)
    for c in (n_steps - 2, n_steps - 1):
        pltpu.make_async_copy(
            down_buf.at[c % 2], down_hbm.at[:, c * step:(c + 1) * step], osem.at[c % 2]
        ).wait()


def expert_math(x_flat, dy_flat, w_gate_e, w_up_e, w_down_e, n_rows, width):
    hid = w_gate_e.shape[1]
    vmem = pl.BlockSpec(memory_space=pltpu.VMEM)
    hbm = pl.BlockSpec(memory_space=pl.ANY)
    row_flat, down_local = pl.pallas_call(
        _expert_kernel,
        out_shape=[
            jax.ShapeDtypeStruct(x_flat.shape, jnp.bfloat16),
            jax.ShapeDtypeStruct((hid, width), jnp.bfloat16),
        ],
        in_specs=[vmem, vmem, hbm, hbm, hbm],
        out_specs=[vmem, hbm],
        scratch_shapes=[
            pltpu.VMEM(w_gate_e.shape, w_gate_e.dtype),
            pltpu.VMEM(w_up_e.shape, w_up_e.dtype),
            pltpu.VMEM(w_down_e.shape, w_down_e.dtype),
            pltpu.VMEM((n_rows, hid), jnp.float32),
            pltpu.VMEM((n_rows, hid), jnp.float32),
            pltpu.VMEM((n_rows, hid), jnp.float32),
            pltpu.VMEM((2, hid, 512), jnp.bfloat16),
            pltpu.VMEM((n_rows, width), jnp.bfloat16),
            pltpu.VMEM((n_rows, width), jnp.bfloat16),
            pltpu.VMEM((x_flat.shape[1] // 128, x_flat.shape[0], 128), jnp.float32),
            pltpu.SemaphoreType.DMA((3, width // 512)),
            pltpu.SemaphoreType.DMA((2,)),
        ],
        compiler_params=pltpu.CompilerParams(vmem_limit_bytes=62 * 1024 * 1024),
    )(x_flat, dy_flat, w_gate_e, w_up_e, w_down_e)
    return (down_local, row_flat)


def body(
    tokens, out_grad, node_lists, expert_local, gate_fixed, gate_weight, up_weight, down_weight
):
    nodes = lax.axis_size("node")
    per_node = lax.axis_size("local")
    experts = nodes * per_node
    tok_dev, top_count = expert_local.shape
    width = tokens.shape[1]
    capacity = tok_dev * top_count // experts
    node_pick = jnp.take_along_axis(node_lists, expert_local // per_node, axis=1)
    expert_ids = (node_pick * per_node + expert_local % per_node).reshape(-1)
    onehot = (expert_ids[:, None] == jnp.arange(experts, dtype=jnp.int32)[None, :]).astype(
        jnp.int32
    )
    running = jnp.cumsum(onehot, axis=0)
    slot = jnp.sum(onehot * running, axis=1) - 1
    kept = slot < capacity
    position = jnp.where(kept, expert_ids * capacity + slot, experts * capacity)
    w_gate_e = gate_weight[0]
    w_up_e = up_weight[0]
    w_down_e = down_weight[0]
    gate_flat = gate_fixed.reshape(-1)
    table = jnp.full((experts * capacity,), -1, jnp.int32)
    table = table.at[position].set(jnp.arange(tok_dev * top_count, dtype=jnp.int32), mode="drop")
    valid = table >= 0
    safe = jnp.maximum(table, 0)
    rows = safe // top_count
    tile_rows = 8
    blocks = tile_rows // capacity
    piece = width // blocks
    slot_token = jnp.where(valid, rows, -1)
    row_key = jnp.where(
        jnp.repeat(valid, blocks),
        jnp.repeat(slot_token, blocks) * blocks + jnp.arange(experts * tile_rows, dtype=jnp.int32) % blocks,
        -1,
    )
    select = (
        row_key[:, None] == jnp.arange(tok_dev * blocks, dtype=jnp.int32)[None, :]
    ).astype(jnp.bfloat16)
    tok_pieces = tokens.reshape(tok_dev * blocks, piece)
    og_pieces = out_grad.reshape(tok_dev * blocks, piece)
    send_x = jnp.dot(select, tok_pieces, preferred_element_type=jnp.float32).astype(jnp.bfloat16)
    gate_val = jnp.where(valid, gate_flat[safe].astype(jnp.float32) * (1.0 / 65536.0), 0.0)
    gate_rows = jnp.repeat(gate_val, blocks)
    og_sel = jnp.dot(select, og_pieces, preferred_element_type=jnp.float32)
    send_dy = (gate_rows[:, None] * og_sel).astype(jnp.bfloat16)
    x_flat, dy_flat = exchange(send_x, send_dy)
    down_local, row_flat = expert_math(
        x_flat, dy_flat, w_gate_e, w_up_e, w_down_e, experts * capacity, width
    )
    (returned,) = exchange(row_flat)
    total = jnp.dot(select.T, returned, preferred_element_type=jnp.float32)
    token_grad = total.reshape(tok_dev, width).astype(jnp.bfloat16)
    return (token_grad, down_local[None])


def solution(mesh):
    return jax.shard_map(
        body,
        mesh=mesh,
        in_specs=(
            P(("node", "local"), None),
            P(("node", "local"), None),
            P(("node", "local"), None),
            P(("node", "local"), None),
            P(("node", "local"), None),
            P(("node", "local"), None, None),
            P(("node", "local"), None, None),
            P(("node", "local"), None, None),
        ),
        out_specs=(P(("node", "local"), None), P(("node", "local"), None, None)),
        check_vma=False,
    )
```

```python
import functools
import jax
import jax.numpy as jnp
from jax import lax
from jax.sharding import PartitionSpec as P
from jax.experimental import pallas as pl
from jax.experimental.pallas import tpu as pltpu


def _exchange_kernel(n_local, *refs):
    count = (len(refs) - 2) // 2
    srcs = refs[:count]
    dsts = refs[count:2 * count]
    send_sems = refs[2 * count]
    recv_sems = refs[2 * count + 1]
    node = lax.axis_index("node")
    local = lax.axis_index("local")
    me = node * n_local + local
    devices = lax.axis_size("node") * n_local
    rows = srcs[0].shape[0] // devices

    def copy_to(p, i):
        return pltpu.make_async_remote_copy(
            src_ref=srcs[i].at[pl.ds(p * rows, rows)],
            dst_ref=dsts[i].at[pl.ds(me * rows, rows)],
            send_sem=send_sems.at[i],
            recv_sem=recv_sems.at[i],
            device_id=(p // n_local, p % n_local),
            device_id_type=pl.DeviceIdType.MESH,
        )

    def local_copy(i):
        return pltpu.make_async_copy(
            srcs[i].at[pl.ds(me * rows, rows)],
            dsts[i].at[pl.ds(me * rows, rows)],
            recv_sems.at[i],
        )

    for i in range(count):
        local_copy(i).start()

    core = node % 2
    y_pos = (node // 2) % 4
    z_pos = node // 8

    def start_body(step, carry):
        t = step % 64
        d_core = step // 64
        dx = t % 4
        dy = (t // 4 + dx) % 4
        dz = (t // 16 + t // 4 + dx) % 4
        node_to = (((z_pos + dz) % 4) * 4 + (y_pos + dy) % 4) * 2 + (core + d_core) % 2
        p = node_to * n_local + (local + dx) % 4
        for i in range(count):
            copy_to(p, i).start()
        return carry

    lax.fori_loop(1, devices, start_body, 0)
    nxt = lax.rem(me + 1, devices)
    for i in range(count):
        pltpu.make_async_copy(dsts[i], dsts[i], recv_sems.at[i]).wait()
        pltpu.make_async_remote_copy(
            src_ref=srcs[i].at[pl.ds(0, (devices - 1) * rows)],
            dst_ref=dsts[i].at[pl.ds(0, (devices - 1) * rows)],
            send_sem=send_sems.at[i],
            recv_sem=recv_sems.at[i],
            device_id=(nxt // n_local, nxt % n_local),
            device_id_type=pl.DeviceIdType.MESH,
        ).wait_send()


def exchange(*arrays):
    n_local = lax.axis_size("local")
    count = len(arrays)
    return pl.pallas_call(
        functools.partial(_exchange_kernel, n_local),
        out_shape=[jax.ShapeDtypeStruct(a.shape, a.dtype) for a in arrays],
        in_specs=[pl.BlockSpec(memory_space=pl.ANY)] * count,
        out_specs=[pl.BlockSpec(memory_space=pl.ANY)] * count,
        scratch_shapes=[
            pltpu.SemaphoreType.DMA((count,)),
            pltpu.SemaphoreType.DMA((count,)),
        ],
        compiler_params=pltpu.CompilerParams(has_side_effects=True),
    )(*arrays)


def _expert_kernel(xf_ref, dyf_ref, wg_hbm, wu_hbm, wd_hbm, row_out, down_hbm,
                   wg, wu, wd, gate_act, up_act, hidden_grad, down_buf, x_ref, dy_ref, wide,
                   wsem, osem):
    k_total = x_ref.shape[1]
    lane = wide.shape[2]
    n_rows = x_ref.shape[0]
    blocks = wide.shape[1] // n_rows
    piece = wide.shape[0] * lane
    for src, dst in ((xf_ref, x_ref), (dyf_ref, dy_ref)):
        for cb in range(wide.shape[0]):
            wide[cb] = src[:, cb * lane:(cb + 1) * lane].astype(jnp.float32)
        for j in range(blocks):
            for cb in range(wide.shape[0]):
                col = j * piece + cb * lane
                dst[:, col:col + lane] = wide[cb, pl.ds(j, n_rows, stride=blocks), :].astype(dst.dtype)
    step = 512
    n_steps = k_total // step
    nt = (((1,), (1,)), ((), ()))
    sources = ((wg_hbm, wg), (wu_hbm, wu))

    def row_chunk(i, k):
        src, dst = sources[i]
        kk = pl.multiple_of(k * step, step)
        return pltpu.make_async_copy(src.at[pl.ds(kk, step)], dst.at[pl.ds(kk, step)], wsem.at[i, k])

    def col_chunk(k):
        kk = pl.multiple_of(k * step, step)
        return pltpu.make_async_copy(wd_hbm.at[:, pl.ds(kk, step)], wd.at[:, pl.ds(kk, step)], wsem.at[2, k])

    def start_body(k, carry):
        row_chunk(0, k).start()
        row_chunk(1, k).start()
        return carry

    lax.fori_loop(0, n_steps, start_body, 0)

    def start_wd(k, carry):
        col_chunk(k).start()
        return carry

    lax.fori_loop(0, n_steps, start_wd, 0)
    gate_act[...] = jnp.zeros(gate_act.shape, gate_act.dtype)
    up_act[...] = jnp.zeros(up_act.shape, up_act.dtype)

    def proj_body(k, carry):
        kk = pl.multiple_of(k * step, step)
        x_blk = x_ref[:, pl.ds(kk, step)]
        row_chunk(0, k).wait()
        gate_act[...] += jnp.dot(x_blk, wg[pl.ds(kk, step), :], preferred_element_type=jnp.float32)
        row_chunk(1, k).wait()
        up_act[...] += jnp.dot(x_blk, wu[pl.ds(kk, step), :], preferred_element_type=jnp.float32)
        return carry

    lax.fori_loop(0, n_steps, proj_body, 0)
    hidden_grad[...] = jnp.zeros(hidden_grad.shape, hidden_grad.dtype)

    def hg_body(k, carry):
        kk = pl.multiple_of(k * step, step)
        col_chunk(k).wait()
        hidden_grad[...] += lax.dot_general(
            dy_ref[:, pl.ds(kk, step)], wd[:, pl.ds(kk, step)], nt,
            preferred_element_type=jnp.float32,
        )
        return carry

    lax.fori_loop(0, n_steps, hg_body, 0)
    g = gate_act[...]
    u = up_act[...]
    hg = hidden_grad[...]
    sig = 1.0 / (1.0 + jnp.exp(-g))
    hidden = (g * sig * u).astype(jnp.bfloat16)
    gate_grad = (hg * u * sig * (1.0 + g * (1.0 - sig))).astype(jnp.bfloat16)
    up_grad = (hg * g * sig).astype(jnp.bfloat16)
    hidden_t = jnp.transpose(hidden.astype(jnp.float32)).astype(jnp.bfloat16)

    for c in range(n_steps):
        cc = c * step
        rg = (
            lax.dot_general(gate_grad, wg[cc:cc + step, :], nt, preferred_element_type=jnp.float32)
            + lax.dot_general(up_grad, wu[cc:cc + step, :], nt, preferred_element_type=jnp.float32)
        ).astype(jnp.bfloat16)
        j, h = divmod(cc, piece)
        for q in range(step // lane):
            wide[h // lane + q, pl.ds(j, n_rows, stride=blocks), :] = (
                rg[:, q * lane:(q + 1) * lane].astype(jnp.float32)
            )
        slot = c % 2
        if c >= 2:
            pltpu.make_async_copy(
                down_buf.at[slot], down_hbm.at[:, cc - 2 * step:cc - step], osem.at[slot]
            ).wait()
        down_buf[slot] = jnp.dot(
            hidden_t, dy_ref[:, cc:cc + step], preferred_element_type=jnp.float32
        ).astype(down_buf.dtype)
        pltpu.make_async_copy(down_buf.at[slot], down_hbm.at[:, cc:cc + step], osem.at[slot]).start()
    for cb in range(wide.shape[0]):
        row_out[:, cb * lane:(cb + 1) * lane] = wide[cb].astype(row_out.dtype)
    for c in (n_steps - 2, n_steps - 1):
        pltpu.make_async_copy(
            down_buf.at[c % 2], down_hbm.at[:, c * step:(c + 1) * step], osem.at[c % 2]
        ).wait()


def expert_math(x_flat, dy_flat, w_gate_e, w_up_e, w_down_e, n_rows, width):
    hid = w_gate_e.shape[1]
    vmem = pl.BlockSpec(memory_space=pltpu.VMEM)
    hbm = pl.BlockSpec(memory_space=pl.ANY)
    row_flat, down_local = pl.pallas_call(
        _expert_kernel,
        out_shape=[
            jax.ShapeDtypeStruct(x_flat.shape, jnp.bfloat16),
            jax.ShapeDtypeStruct((hid, width), jnp.bfloat16),
        ],
        in_specs=[vmem, vmem, hbm, hbm, hbm],
        out_specs=[vmem, hbm],
        scratch_shapes=[
            pltpu.VMEM(w_gate_e.shape, w_gate_e.dtype),
            pltpu.VMEM(w_up_e.shape, w_up_e.dtype),
            pltpu.VMEM(w_down_e.shape, w_down_e.dtype),
            pltpu.VMEM((n_rows, hid), jnp.float32),
            pltpu.VMEM((n_rows, hid), jnp.float32),
            pltpu.VMEM((n_rows, hid), jnp.float32),
            pltpu.VMEM((2, hid, 512), jnp.bfloat16),
            pltpu.VMEM((n_rows, width), jnp.bfloat16),
            pltpu.VMEM((n_rows, width), jnp.bfloat16),
            pltpu.VMEM((x_flat.shape[1] // 128, x_flat.shape[0], 128), jnp.float32),
            pltpu.SemaphoreType.DMA((3, width // 512)),
            pltpu.SemaphoreType.DMA((2,)),
        ],
        compiler_params=pltpu.CompilerParams(vmem_limit_bytes=62 * 1024 * 1024),
    )(x_flat, dy_flat, w_gate_e, w_up_e, w_down_e)
    return (down_local, row_flat)


def body(
    tokens, out_grad, node_lists, expert_local, gate_fixed, gate_weight, up_weight, down_weight
):
    nodes = lax.axis_size("node")
    per_node = lax.axis_size("local")
    experts = nodes * per_node
    tok_dev, top_count = expert_local.shape
    width = tokens.shape[1]
    capacity = tok_dev * top_count // experts
    group_pos = expert_local // per_node
    node_pick = jnp.zeros_like(expert_local)
    for k in range(node_lists.shape[1]):
        node_pick = node_pick + jnp.where(group_pos == k, node_lists[:, k:k + 1], 0)
    expert_ids = (node_pick * per_node + expert_local % per_node).reshape(-1)
    onehot = (expert_ids[:, None] == jnp.arange(experts, dtype=jnp.int32)[None, :]).astype(
        jnp.int32
    )
    running = jnp.cumsum(onehot, axis=0)
    slot = jnp.sum(onehot * running, axis=1) - 1
    kept = slot < capacity
    position = jnp.where(kept, expert_ids * capacity + slot, experts * capacity)
    w_gate_e = gate_weight[0]
    w_up_e = up_weight[0]
    w_down_e = down_weight[0]
    gate_flat = gate_fixed.reshape(-1)
    fills = position[:, None] == jnp.arange(experts * capacity, dtype=jnp.int32)[None, :]
    valid = jnp.any(fills, axis=0)
    assign_ids = jnp.arange(tok_dev * top_count, dtype=jnp.int32)[:, None]
    rows = jnp.sum(jnp.where(fills, assign_ids // top_count, 0), axis=0)
    gate_slot = jnp.sum(jnp.where(fills, gate_flat[:, None], 0), axis=0)
    tile_rows = 8
    blocks = tile_rows // capacity
    piece = width // blocks
    slot_token = jnp.where(valid, rows, -1)
    row_key = jnp.where(
        jnp.repeat(valid, blocks),
        jnp.repeat(slot_token, blocks) * blocks + jnp.arange(experts * tile_rows, dtype=jnp.int32) % blocks,
        -1,
    )
    select = (
        row_key[:, None] == jnp.arange(tok_dev * blocks, dtype=jnp.int32)[None, :]
    ).astype(jnp.bfloat16)
    tok_pieces = tokens.reshape(tok_dev * blocks, piece)
    og_pieces = out_grad.reshape(tok_dev * blocks, piece)
    send_x = jnp.dot(select, tok_pieces, preferred_element_type=jnp.float32).astype(jnp.bfloat16)
    gate_val = jnp.where(valid, gate_slot.astype(jnp.float32) * (1.0 / 65536.0), 0.0)
    gate_rows = jnp.repeat(gate_val, blocks)
    og_sel = jnp.dot(select, og_pieces, preferred_element_type=jnp.float32)
    send_dy = (gate_rows[:, None] * og_sel).astype(jnp.bfloat16)
    x_flat, dy_flat = exchange(send_x, send_dy)
    down_local, row_flat = expert_math(
        x_flat, dy_flat, w_gate_e, w_up_e, w_down_e, experts * capacity, width
    )
    (returned,) = exchange(row_flat)
    total = jnp.dot(select.T, returned, preferred_element_type=jnp.float32)
    token_grad = total.reshape(tok_dev, width).astype(jnp.bfloat16)
    return (token_grad, down_local[None])


def solution(mesh):
    return jax.shard_map(
        body,
        mesh=mesh,
        in_specs=(
            P(("node", "local"), None),
            P(("node", "local"), None),
            P(("node", "local"), None),
            P(("node", "local"), None),
            P(("node", "local"), None),
            P(("node", "local"), None, None),
            P(("node", "local"), None, None),
            P(("node", "local"), None, None),
        ),
        out_specs=(P(("node", "local"), None), P(("node", "local"), None, None)),
        check_vma=False,
    )
```

```python
import functools
import jax
import jax.numpy as jnp
from jax import lax
from jax.sharding import PartitionSpec as P
from jax.experimental import pallas as pl
from jax.experimental.pallas import tpu as pltpu


def _exchange_kernel(n_local, *refs):
    count = (len(refs) - 2) // 2
    srcs = refs[:count]
    dsts = refs[count:2 * count]
    send_sems = refs[2 * count]
    recv_sems = refs[2 * count + 1]
    node = lax.axis_index("node")
    local = lax.axis_index("local")
    me = node * n_local + local
    devices = lax.axis_size("node") * n_local
    rows = srcs[0].shape[0] // devices

    def copy_to(p, i):
        return pltpu.make_async_remote_copy(
            src_ref=srcs[i].at[pl.ds(p * rows, rows)],
            dst_ref=dsts[i].at[pl.ds(me * rows, rows)],
            send_sem=send_sems.at[i],
            recv_sem=recv_sems.at[i],
            device_id=(p // n_local, p % n_local),
            device_id_type=pl.DeviceIdType.MESH,
        )

    def local_copy(i):
        return pltpu.make_async_copy(
            srcs[i].at[pl.ds(me * rows, rows)],
            dsts[i].at[pl.ds(me * rows, rows)],
            recv_sems.at[i],
        )

    for i in range(count):
        local_copy(i).start()

    core = node % 2
    y_pos = (node // 2) % 4
    z_pos = node // 8

    def start_body(step, carry):
        t = step % 64
        d_core = step // 64
        dx = t % 4
        dy = (t // 4 + dx) % 4
        dz = (t // 16 + t // 4 + dx) % 4
        node_to = (((z_pos + dz) % 4) * 4 + (y_pos + dy) % 4) * 2 + (core + d_core) % 2
        p = node_to * n_local + (local + dx) % 4
        for i in range(count):
            copy_to(p, i).start()
        return carry

    lax.fori_loop(1, devices, start_body, 0)
    nxt = lax.rem(me + 1, devices)
    for i in range(count):
        pltpu.make_async_copy(dsts[i], dsts[i], recv_sems.at[i]).wait()
        pltpu.make_async_remote_copy(
            src_ref=srcs[i].at[pl.ds(0, (devices - 1) * rows)],
            dst_ref=dsts[i].at[pl.ds(0, (devices - 1) * rows)],
            send_sem=send_sems.at[i],
            recv_sem=recv_sems.at[i],
            device_id=(nxt // n_local, nxt % n_local),
            device_id_type=pl.DeviceIdType.MESH,
        ).wait_send()


def exchange(*arrays):
    n_local = lax.axis_size("local")
    count = len(arrays)
    return pl.pallas_call(
        functools.partial(_exchange_kernel, n_local),
        out_shape=[jax.ShapeDtypeStruct(a.shape, a.dtype) for a in arrays],
        in_specs=[pl.BlockSpec(memory_space=pl.ANY)] * count,
        out_specs=[pl.BlockSpec(memory_space=pl.ANY)] * count,
        scratch_shapes=[
            pltpu.SemaphoreType.DMA((count,)),
            pltpu.SemaphoreType.DMA((count,)),
        ],
        compiler_params=pltpu.CompilerParams(has_side_effects=True),
    )(*arrays)


def _expert_kernel(xf_ref, dyf_ref, wg_hbm, wu_hbm, wd_hbm, row_out, down_hbm,
                   wg, wu, wd, gate_act, up_act, hidden_grad, down_buf, x_ref, dy_ref, wide,
                   wsem, osem):
    k_total = x_ref.shape[1]
    lane = wide.shape[2]
    n_rows = x_ref.shape[0]
    blocks = wide.shape[1] // n_rows
    piece = wide.shape[0] * lane
    for src, dst in ((xf_ref, x_ref), (dyf_ref, dy_ref)):
        for cb in range(wide.shape[0]):
            wide[cb] = src[:, cb * lane:(cb + 1) * lane].astype(jnp.float32)
        for j in range(blocks):
            for cb in range(wide.shape[0]):
                col = j * piece + cb * lane
                dst[:, col:col + lane] = wide[cb, pl.ds(j, n_rows, stride=blocks), :].astype(dst.dtype)
    step = 1024
    n_steps = k_total // step
    nt = (((1,), (1,)), ((), ()))
    sources = ((wg_hbm, wg), (wu_hbm, wu))

    def row_chunk(i, k):
        src, dst = sources[i]
        kk = pl.multiple_of(k * step, step)
        return pltpu.make_async_copy(src.at[pl.ds(kk, step)], dst.at[pl.ds(kk, step)], wsem.at[i, k])

    def col_chunk(k):
        kk = pl.multiple_of(k * step, step)
        return pltpu.make_async_copy(wd_hbm.at[:, pl.ds(kk, step)], wd.at[:, pl.ds(kk, step)], wsem.at[2, k])

    def start_body(k, carry):
        row_chunk(0, k).start()
        row_chunk(1, k).start()
        return carry

    lax.fori_loop(0, n_steps, start_body, 0)

    def start_wd(k, carry):
        col_chunk(k).start()
        return carry

    lax.fori_loop(0, n_steps, start_wd, 0)
    gate_act[...] = jnp.zeros(gate_act.shape, gate_act.dtype)
    up_act[...] = jnp.zeros(up_act.shape, up_act.dtype)

    def proj_body(k, carry):
        kk = pl.multiple_of(k * step, step)
        x_blk = x_ref[:, pl.ds(kk, step)]
        row_chunk(0, k).wait()
        gate_act[...] += jnp.dot(x_blk, wg[pl.ds(kk, step), :], preferred_element_type=jnp.float32)
        row_chunk(1, k).wait()
        up_act[...] += jnp.dot(x_blk, wu[pl.ds(kk, step), :], preferred_element_type=jnp.float32)
        return carry

    lax.fori_loop(0, n_steps, proj_body, 0)
    hidden_grad[...] = jnp.zeros(hidden_grad.shape, hidden_grad.dtype)

    def hg_body(k, carry):
        kk = pl.multiple_of(k * step, step)
        col_chunk(k).wait()
        hidden_grad[...] += lax.dot_general(
            dy_ref[:, pl.ds(kk, step)], wd[:, pl.ds(kk, step)], nt,
            preferred_element_type=jnp.float32,
        )
        return carry

    lax.fori_loop(0, n_steps, hg_body, 0)
    g = gate_act[...]
    u = up_act[...]
    hg = hidden_grad[...]
    sig = 1.0 / (1.0 + jnp.exp(-g))
    hidden = (g * sig * u).astype(jnp.bfloat16)
    gate_grad = (hg * u * sig * (1.0 + g * (1.0 - sig))).astype(jnp.bfloat16)
    up_grad = (hg * g * sig).astype(jnp.bfloat16)
    hidden_t = jnp.transpose(hidden.astype(jnp.float32)).astype(jnp.bfloat16)

    for c in range(n_steps):
        cc = c * step
        rg = (
            lax.dot_general(gate_grad, wg[cc:cc + step, :], nt, preferred_element_type=jnp.float32)
            + lax.dot_general(up_grad, wu[cc:cc + step, :], nt, preferred_element_type=jnp.float32)
        ).astype(jnp.bfloat16)
        j, h = divmod(cc, piece)
        for q in range(step // lane):
            wide[h // lane + q, pl.ds(j, n_rows, stride=blocks), :] = (
                rg[:, q * lane:(q + 1) * lane].astype(jnp.float32)
            )
        slot = c % 2
        if c >= 2:
            pltpu.make_async_copy(
                down_buf.at[slot], down_hbm.at[:, cc - 2 * step:cc - step], osem.at[slot]
            ).wait()
        down_buf[slot] = jnp.dot(
            hidden_t, dy_ref[:, cc:cc + step], preferred_element_type=jnp.float32
        ).astype(down_buf.dtype)
        pltpu.make_async_copy(down_buf.at[slot], down_hbm.at[:, cc:cc + step], osem.at[slot]).start()
    for cb in range(wide.shape[0]):
        row_out[:, cb * lane:(cb + 1) * lane] = wide[cb].astype(row_out.dtype)
    for c in (n_steps - 2, n_steps - 1):
        pltpu.make_async_copy(
            down_buf.at[c % 2], down_hbm.at[:, c * step:(c + 1) * step], osem.at[c % 2]
        ).wait()


def expert_math(x_flat, dy_flat, w_gate_e, w_up_e, w_down_e, n_rows, width):
    hid = w_gate_e.shape[1]
    vmem = pl.BlockSpec(memory_space=pltpu.VMEM)
    hbm = pl.BlockSpec(memory_space=pl.ANY)
    row_flat, down_local = pl.pallas_call(
        _expert_kernel,
        out_shape=[
            jax.ShapeDtypeStruct(x_flat.shape, jnp.bfloat16),
            jax.ShapeDtypeStruct((hid, width), jnp.bfloat16),
        ],
        in_specs=[vmem, vmem, hbm, hbm, hbm],
        out_specs=[vmem, hbm],
        scratch_shapes=[
            pltpu.VMEM(w_gate_e.shape, w_gate_e.dtype),
            pltpu.VMEM(w_up_e.shape, w_up_e.dtype),
            pltpu.VMEM(w_down_e.shape, w_down_e.dtype),
            pltpu.VMEM((n_rows, hid), jnp.float32),
            pltpu.VMEM((n_rows, hid), jnp.float32),
            pltpu.VMEM((n_rows, hid), jnp.float32),
            pltpu.VMEM((2, hid, 1024), jnp.bfloat16),
            pltpu.VMEM((n_rows, width), jnp.bfloat16),
            pltpu.VMEM((n_rows, width), jnp.bfloat16),
            pltpu.VMEM((x_flat.shape[1] // 128, x_flat.shape[0], 128), jnp.float32),
            pltpu.SemaphoreType.DMA((3, width // 1024)),
            pltpu.SemaphoreType.DMA((2,)),
        ],
        compiler_params=pltpu.CompilerParams(vmem_limit_bytes=62 * 1024 * 1024),
    )(x_flat, dy_flat, w_gate_e, w_up_e, w_down_e)
    return (down_local, row_flat)


def body(
    tokens, out_grad, node_lists, expert_local, gate_fixed, gate_weight, up_weight, down_weight
):
    nodes = lax.axis_size("node")
    per_node = lax.axis_size("local")
    experts = nodes * per_node
    tok_dev, top_count = expert_local.shape
    width = tokens.shape[1]
    capacity = tok_dev * top_count // experts
    group_pos = expert_local // per_node
    node_pick = jnp.zeros_like(expert_local)
    for k in range(node_lists.shape[1]):
        node_pick = node_pick + jnp.where(group_pos == k, node_lists[:, k:k + 1], 0)
    expert_ids = (node_pick * per_node + expert_local % per_node).reshape(-1)
    onehot = (expert_ids[:, None] == jnp.arange(experts, dtype=jnp.int32)[None, :]).astype(
        jnp.int32
    )
    running = jnp.cumsum(onehot, axis=0)
    slot = jnp.sum(onehot * running, axis=1) - 1
    kept = slot < capacity
    position = jnp.where(kept, expert_ids * capacity + slot, experts * capacity)
    w_gate_e = gate_weight[0]
    w_up_e = up_weight[0]
    w_down_e = down_weight[0]
    gate_flat = gate_fixed.reshape(-1)
    fills = position[:, None] == jnp.arange(experts * capacity, dtype=jnp.int32)[None, :]
    valid = jnp.any(fills, axis=0)
    assign_ids = jnp.arange(tok_dev * top_count, dtype=jnp.int32)[:, None]
    rows = jnp.sum(jnp.where(fills, assign_ids // top_count, 0), axis=0)
    gate_slot = jnp.sum(jnp.where(fills, gate_flat[:, None], 0), axis=0)
    tile_rows = 8
    blocks = tile_rows // capacity
    piece = width // blocks
    slot_token = jnp.where(valid, rows, -1)
    row_key = jnp.where(
        jnp.repeat(valid, blocks),
        jnp.repeat(slot_token, blocks) * blocks + jnp.arange(experts * tile_rows, dtype=jnp.int32) % blocks,
        -1,
    )
    select = (
        row_key[:, None] == jnp.arange(tok_dev * blocks, dtype=jnp.int32)[None, :]
    ).astype(jnp.bfloat16)
    tok_pieces = tokens.reshape(tok_dev * blocks, piece)
    og_pieces = out_grad.reshape(tok_dev * blocks, piece)
    send_x = jnp.dot(select, tok_pieces, preferred_element_type=jnp.float32).astype(jnp.bfloat16)
    gate_val = jnp.where(valid, gate_slot.astype(jnp.float32) * (1.0 / 65536.0), 0.0)
    gate_rows = jnp.repeat(gate_val, blocks)
    og_sel = jnp.dot(select, og_pieces, preferred_element_type=jnp.float32)
    send_dy = (gate_rows[:, None] * og_sel).astype(jnp.bfloat16)
    x_flat, dy_flat = exchange(send_x, send_dy)
    down_local, row_flat = expert_math(
        x_flat, dy_flat, w_gate_e, w_up_e, w_down_e, experts * capacity, width
    )
    (returned,) = exchange(row_flat)
    total = jnp.dot(select.T, returned, preferred_element_type=jnp.float32)
    token_grad = total.reshape(tok_dev, width).astype(jnp.bfloat16)
    return (token_grad, down_local[None])


def solution(mesh):
    return jax.shard_map(
        body,
        mesh=mesh,
        in_specs=(
            P(("node", "local"), None),
            P(("node", "local"), None),
            P(("node", "local"), None),
            P(("node", "local"), None),
            P(("node", "local"), None),
            P(("node", "local"), None, None),
            P(("node", "local"), None, None),
            P(("node", "local"), None, None),
        ),
        out_specs=(P(("node", "local"), None), P(("node", "local"), None, None)),
        check_vma=False,
    )
```

```python
import functools
import jax
import jax.numpy as jnp
from jax import lax
from jax.sharding import PartitionSpec as P
from jax.experimental import pallas as pl
from jax.experimental.pallas import tpu as pltpu


def _exchange_kernel(n_local, *refs):
    count = (len(refs) - 2) // 2
    srcs = refs[:count]
    dsts = refs[count:2 * count]
    send_sems = refs[2 * count]
    recv_sems = refs[2 * count + 1]
    node = lax.axis_index("node")
    local = lax.axis_index("local")
    me = node * n_local + local
    devices = lax.axis_size("node") * n_local
    rows = srcs[0].shape[0] // devices

    def copy_to(p, i):
        return pltpu.make_async_remote_copy(
            src_ref=srcs[i].at[pl.ds(p * rows, rows)],
            dst_ref=dsts[i].at[pl.ds(me * rows, rows)],
            send_sem=send_sems.at[i],
            recv_sem=recv_sems.at[i],
            device_id=(p // n_local, p % n_local),
            device_id_type=pl.DeviceIdType.MESH,
        )

    def local_copy(i):
        return pltpu.make_async_copy(
            srcs[i].at[pl.ds(me * rows, rows)],
            dsts[i].at[pl.ds(me * rows, rows)],
            recv_sems.at[i],
        )

    for i in range(count):
        local_copy(i).start()

    core = node % 2
    y_pos = (node // 2) % 4
    z_pos = node // 8

    def start_body(step, carry):
        t = step % 64
        d_core = step // 64
        dx = t % 4
        dy = (t // 4 + dx) % 4
        dz = (t // 16 + t // 4 + dx) % 4
        node_to = (((z_pos + dz) % 4) * 4 + (y_pos + dy) % 4) * 2 + (core + d_core) % 2
        p = node_to * n_local + (local + dx) % 4
        for i in range(count):
            copy_to(p, i).start()
        return carry

    lax.fori_loop(1, devices, start_body, 0)
    nxt = lax.rem(me + 1, devices)
    for i in range(count):
        pltpu.make_async_copy(dsts[i], dsts[i], recv_sems.at[i]).wait()
        pltpu.make_async_remote_copy(
            src_ref=srcs[i].at[pl.ds(0, (devices - 1) * rows)],
            dst_ref=dsts[i].at[pl.ds(0, (devices - 1) * rows)],
            send_sem=send_sems.at[i],
            recv_sem=recv_sems.at[i],
            device_id=(nxt // n_local, nxt % n_local),
            device_id_type=pl.DeviceIdType.MESH,
        ).wait_send()


def exchange(*arrays):
    n_local = lax.axis_size("local")
    count = len(arrays)
    return pl.pallas_call(
        functools.partial(_exchange_kernel, n_local),
        out_shape=[jax.ShapeDtypeStruct(a.shape, a.dtype) for a in arrays],
        in_specs=[pl.BlockSpec(memory_space=pl.ANY)] * count,
        out_specs=[pl.BlockSpec(memory_space=pl.ANY)] * count,
        scratch_shapes=[
            pltpu.SemaphoreType.DMA((count,)),
            pltpu.SemaphoreType.DMA((count,)),
        ],
        compiler_params=pltpu.CompilerParams(has_side_effects=True),
    )(*arrays)


def _expert_kernel(xf_ref, dyf_ref, wg_hbm, wu_hbm, wd_hbm, row_out, down_hbm,
                   wg, wu, wd, gate_act, up_act, hidden_grad, down_buf, x_ref, dy_ref, wide,
                   wsem, osem):
    k_total = x_ref.shape[1]
    lane = wide.shape[2]
    n_rows = x_ref.shape[0]
    blocks = wide.shape[1] // n_rows
    piece = wide.shape[0] * lane
    for src, dst in ((xf_ref, x_ref), (dyf_ref, dy_ref)):
        for cb in range(wide.shape[0]):
            wide[cb] = src[:, cb * lane:(cb + 1) * lane].astype(jnp.float32)
        for j in range(blocks):
            for cb in range(wide.shape[0]):
                col = j * piece + cb * lane
                dst[:, col:col + lane] = wide[cb, pl.ds(j, n_rows, stride=blocks), :].astype(dst.dtype)
    step = 2048
    n_steps = k_total // step
    nt = (((1,), (1,)), ((), ()))
    sources = ((wg_hbm, wg), (wu_hbm, wu))

    def row_chunk(i, k):
        src, dst = sources[i]
        kk = pl.multiple_of(k * step, step)
        return pltpu.make_async_copy(src.at[pl.ds(kk, step)], dst.at[pl.ds(kk, step)], wsem.at[i, k])

    def col_chunk(k):
        kk = pl.multiple_of(k * step, step)
        return pltpu.make_async_copy(wd_hbm.at[:, pl.ds(kk, step)], wd.at[:, pl.ds(kk, step)], wsem.at[2, k])

    def start_body(k, carry):
        row_chunk(0, k).start()
        row_chunk(1, k).start()
        return carry

    lax.fori_loop(0, n_steps, start_body, 0)

    def start_wd(k, carry):
        col_chunk(k).start()
        return carry

    lax.fori_loop(0, n_steps, start_wd, 0)
    gate_act[...] = jnp.zeros(gate_act.shape, gate_act.dtype)
    up_act[...] = jnp.zeros(up_act.shape, up_act.dtype)

    def proj_body(k, carry):
        kk = pl.multiple_of(k * step, step)
        x_blk = x_ref[:, pl.ds(kk, step)]
        row_chunk(0, k).wait()
        gate_act[...] += jnp.dot(x_blk, wg[pl.ds(kk, step), :], preferred_element_type=jnp.float32)
        row_chunk(1, k).wait()
        up_act[...] += jnp.dot(x_blk, wu[pl.ds(kk, step), :], preferred_element_type=jnp.float32)
        return carry

    lax.fori_loop(0, n_steps, proj_body, 0)
    hidden_grad[...] = jnp.zeros(hidden_grad.shape, hidden_grad.dtype)

    def hg_body(k, carry):
        kk = pl.multiple_of(k * step, step)
        col_chunk(k).wait()
        hidden_grad[...] += lax.dot_general(
            dy_ref[:, pl.ds(kk, step)], wd[:, pl.ds(kk, step)], nt,
            preferred_element_type=jnp.float32,
        )
        return carry

    lax.fori_loop(0, n_steps, hg_body, 0)
    g = gate_act[...]
    u = up_act[...]
    hg = hidden_grad[...]
    sig = 1.0 / (1.0 + jnp.exp(-g))
    hidden = (g * sig * u).astype(jnp.bfloat16)
    gate_grad = (hg * u * sig * (1.0 + g * (1.0 - sig))).astype(jnp.bfloat16)
    up_grad = (hg * g * sig).astype(jnp.bfloat16)
    hidden_t = jnp.transpose(hidden.astype(jnp.float32)).astype(jnp.bfloat16)

    for c in range(n_steps):
        cc = c * step
        rg = (
            lax.dot_general(gate_grad, wg[cc:cc + step, :], nt, preferred_element_type=jnp.float32)
            + lax.dot_general(up_grad, wu[cc:cc + step, :], nt, preferred_element_type=jnp.float32)
        ).astype(jnp.bfloat16)
        for q in range(step // lane):
            j, h = divmod(cc + q * lane, piece)
            wide[h // lane, pl.ds(j, n_rows, stride=blocks), :] = (
                rg[:, q * lane:(q + 1) * lane].astype(jnp.float32)
            )
        slot = c % 2
        if c >= 2:
            pltpu.make_async_copy(
                down_buf.at[slot], down_hbm.at[:, cc - 2 * step:cc - step], osem.at[slot]
            ).wait()
        down_buf[slot] = jnp.dot(
            hidden_t, dy_ref[:, cc:cc + step], preferred_element_type=jnp.float32
        ).astype(down_buf.dtype)
        pltpu.make_async_copy(down_buf.at[slot], down_hbm.at[:, cc:cc + step], osem.at[slot]).start()
    for cb in range(wide.shape[0]):
        row_out[:, cb * lane:(cb + 1) * lane] = wide[cb].astype(row_out.dtype)
    for c in (n_steps - 2, n_steps - 1):
        pltpu.make_async_copy(
            down_buf.at[c % 2], down_hbm.at[:, c * step:(c + 1) * step], osem.at[c % 2]
        ).wait()


def expert_math(x_flat, dy_flat, w_gate_e, w_up_e, w_down_e, n_rows, width):
    hid = w_gate_e.shape[1]
    vmem = pl.BlockSpec(memory_space=pltpu.VMEM)
    hbm = pl.BlockSpec(memory_space=pl.ANY)
    row_flat, down_local = pl.pallas_call(
        _expert_kernel,
        out_shape=[
            jax.ShapeDtypeStruct(x_flat.shape, jnp.bfloat16),
            jax.ShapeDtypeStruct((hid, width), jnp.bfloat16),
        ],
        in_specs=[vmem, vmem, hbm, hbm, hbm],
        out_specs=[vmem, hbm],
        scratch_shapes=[
            pltpu.VMEM(w_gate_e.shape, w_gate_e.dtype),
            pltpu.VMEM(w_up_e.shape, w_up_e.dtype),
            pltpu.VMEM(w_down_e.shape, w_down_e.dtype),
            pltpu.VMEM((n_rows, hid), jnp.float32),
            pltpu.VMEM((n_rows, hid), jnp.float32),
            pltpu.VMEM((n_rows, hid), jnp.float32),
            pltpu.VMEM((2, hid, 2048), jnp.bfloat16),
            pltpu.VMEM((n_rows, width), jnp.bfloat16),
            pltpu.VMEM((n_rows, width), jnp.bfloat16),
            pltpu.VMEM((x_flat.shape[1] // 128, x_flat.shape[0], 128), jnp.float32),
            pltpu.SemaphoreType.DMA((3, width // 2048)),
            pltpu.SemaphoreType.DMA((2,)),
        ],
        compiler_params=pltpu.CompilerParams(vmem_limit_bytes=62 * 1024 * 1024),
    )(x_flat, dy_flat, w_gate_e, w_up_e, w_down_e)
    return (down_local, row_flat)


def body(
    tokens, out_grad, node_lists, expert_local, gate_fixed, gate_weight, up_weight, down_weight
):
    nodes = lax.axis_size("node")
    per_node = lax.axis_size("local")
    experts = nodes * per_node
    tok_dev, top_count = expert_local.shape
    width = tokens.shape[1]
    capacity = tok_dev * top_count // experts
    group_pos = expert_local // per_node
    node_pick = jnp.zeros_like(expert_local)
    for k in range(node_lists.shape[1]):
        node_pick = node_pick + jnp.where(group_pos == k, node_lists[:, k:k + 1], 0)
    expert_ids = (node_pick * per_node + expert_local % per_node).reshape(-1)
    onehot = (expert_ids[:, None] == jnp.arange(experts, dtype=jnp.int32)[None, :]).astype(
        jnp.int32
    )
    running = jnp.cumsum(onehot, axis=0)
    slot = jnp.sum(onehot * running, axis=1) - 1
    kept = slot < capacity
    position = jnp.where(kept, expert_ids * capacity + slot, experts * capacity)
    w_gate_e = gate_weight[0]
    w_up_e = up_weight[0]
    w_down_e = down_weight[0]
    gate_flat = gate_fixed.reshape(-1)
    fills = position[:, None] == jnp.arange(experts * capacity, dtype=jnp.int32)[None, :]
    valid = jnp.any(fills, axis=0)
    assign_ids = jnp.arange(tok_dev * top_count, dtype=jnp.int32)[:, None]
    rows = jnp.sum(jnp.where(fills, assign_ids // top_count, 0), axis=0)
    gate_slot = jnp.sum(jnp.where(fills, gate_flat[:, None], 0), axis=0)
    tile_rows = 8
    blocks = tile_rows // capacity
    piece = width // blocks
    slot_token = jnp.where(valid, rows, -1)
    row_key = jnp.where(
        jnp.repeat(valid, blocks),
        jnp.repeat(slot_token, blocks) * blocks + jnp.arange(experts * tile_rows, dtype=jnp.int32) % blocks,
        -1,
    )
    select = (
        row_key[:, None] == jnp.arange(tok_dev * blocks, dtype=jnp.int32)[None, :]
    ).astype(jnp.bfloat16)
    tok_pieces = tokens.reshape(tok_dev * blocks, piece)
    og_pieces = out_grad.reshape(tok_dev * blocks, piece)
    send_x = jnp.dot(select, tok_pieces, preferred_element_type=jnp.float32).astype(jnp.bfloat16)
    gate_val = jnp.where(valid, gate_slot.astype(jnp.float32) * (1.0 / 65536.0), 0.0)
    gate_rows = jnp.repeat(gate_val, blocks)
    og_sel = jnp.dot(select, og_pieces, preferred_element_type=jnp.float32)
    send_dy = (gate_rows[:, None] * og_sel).astype(jnp.bfloat16)
    x_flat, dy_flat = exchange(send_x, send_dy)
    down_local, row_flat = expert_math(
        x_flat, dy_flat, w_gate_e, w_up_e, w_down_e, experts * capacity, width
    )
    (returned,) = exchange(row_flat)
    total = jnp.dot(select.T, returned, preferred_element_type=jnp.float32)
    token_grad = total.reshape(tok_dev, width).astype(jnp.bfloat16)
    return (token_grad, down_local[None])


def solution(mesh):
    return jax.shard_map(
        body,
        mesh=mesh,
        in_specs=(
            P(("node", "local"), None),
            P(("node", "local"), None),
            P(("node", "local"), None),
            P(("node", "local"), None),
            P(("node", "local"), None),
            P(("node", "local"), None, None),
            P(("node", "local"), None, None),
            P(("node", "local"), None, None),
        ),
        out_specs=(P(("node", "local"), None), P(("node", "local"), None, None)),
        check_vma=False,
    )
```

```python
import functools
import jax
import jax.numpy as jnp
from jax import lax
from jax.sharding import PartitionSpec as P
from jax.experimental import pallas as pl
from jax.experimental.pallas import tpu as pltpu


def _exchange_kernel(n_local, *refs):
    count = (len(refs) - 2) // 2
    srcs = refs[:count]
    dsts = refs[count:2 * count]
    send_sems = refs[2 * count]
    recv_sems = refs[2 * count + 1]
    node = lax.axis_index("node")
    local = lax.axis_index("local")
    me = node * n_local + local
    devices = lax.axis_size("node") * n_local
    rows = srcs[0].shape[0] // devices

    def copy_to(p, i):
        return pltpu.make_async_remote_copy(
            src_ref=srcs[i].at[pl.ds(p * rows, rows)],
            dst_ref=dsts[i].at[pl.ds(me * rows, rows)],
            send_sem=send_sems.at[i],
            recv_sem=recv_sems.at[i],
            device_id=(p // n_local, p % n_local),
            device_id_type=pl.DeviceIdType.MESH,
        )

    def local_copy(i):
        return pltpu.make_async_copy(
            srcs[i].at[pl.ds(me * rows, rows)],
            dsts[i].at[pl.ds(me * rows, rows)],
            recv_sems.at[i],
        )

    for i in range(count):
        local_copy(i).start()

    core = node % 2
    y_pos = (node // 2) % 4
    z_pos = node // 8

    def start_body(step, carry):
        t = step % 64
        d_core = step // 64
        dx = t % 4
        dy = (t // 4 + dx) % 4
        dz = (t // 16 + t // 4 + dx) % 4
        node_to = (((z_pos + dz) % 4) * 4 + (y_pos + dy) % 4) * 2 + (core + d_core) % 2
        p = node_to * n_local + (local + dx) % 4
        for i in range(count):
            copy_to(p, i).start()
        return carry

    lax.fori_loop(1, devices, start_body, 0)
    nxt = lax.rem(me + 1, devices)
    for i in range(count):
        pltpu.make_async_copy(dsts[i], dsts[i], recv_sems.at[i]).wait()
        pltpu.make_async_remote_copy(
            src_ref=srcs[i].at[pl.ds(0, (devices - 1) * rows)],
            dst_ref=dsts[i].at[pl.ds(0, (devices - 1) * rows)],
            send_sem=send_sems.at[i],
            recv_sem=recv_sems.at[i],
            device_id=(nxt // n_local, nxt % n_local),
            device_id_type=pl.DeviceIdType.MESH,
        ).wait_send()


def exchange(*arrays):
    n_local = lax.axis_size("local")
    count = len(arrays)
    return pl.pallas_call(
        functools.partial(_exchange_kernel, n_local),
        out_shape=[jax.ShapeDtypeStruct(a.shape, a.dtype) for a in arrays],
        in_specs=[pl.BlockSpec(memory_space=pl.ANY)] * count,
        out_specs=[pl.BlockSpec(memory_space=pl.ANY)] * count,
        scratch_shapes=[
            pltpu.SemaphoreType.DMA((count,)),
            pltpu.SemaphoreType.DMA((count,)),
        ],
        compiler_params=pltpu.CompilerParams(has_side_effects=True),
    )(*arrays)


def _expert_kernel(xf_ref, dyf_ref, wg_hbm, wu_hbm, wd_hbm, row_out, down_hbm,
                   wg, wu, wd, gate_act, up_act, hidden_grad, down_buf, x_ref, dy_ref, wide,
                   wsem, osem):
    k_total = x_ref.shape[1]
    lane = wide.shape[2]
    n_rows = x_ref.shape[0]
    blocks = wide.shape[1] // n_rows
    piece = wide.shape[0] * lane
    for src, dst in ((xf_ref, x_ref), (dyf_ref, dy_ref)):
        for cb in range(wide.shape[0]):
            wide[cb] = src[:, cb * lane:(cb + 1) * lane].astype(jnp.float32)
        for j in range(blocks):
            for cb in range(wide.shape[0]):
                col = j * piece + cb * lane
                dst[:, col:col + lane] = wide[cb, pl.ds(j, n_rows, stride=blocks), :].astype(dst.dtype)
    step = 2048
    n_steps = k_total // step
    nt = (((1,), (1,)), ((), ()))
    sources = ((wg_hbm, wg), (wu_hbm, wu))

    def row_chunk(i, k):
        src, dst = sources[i]
        kk = pl.multiple_of(k * step, step)
        return pltpu.make_async_copy(src.at[pl.ds(kk, step)], dst.at[pl.ds(kk, step)], wsem.at[i, k])

    def col_chunk(k):
        kk = pl.multiple_of(k * step, step)
        return pltpu.make_async_copy(wd_hbm.at[:, pl.ds(kk, step)], wd.at[:, pl.ds(kk, step)], wsem.at[2, k])

    def start_body(k, carry):
        row_chunk(0, k).start()
        row_chunk(1, k).start()
        return carry

    lax.fori_loop(0, n_steps, start_body, 0)

    def start_wd(k, carry):
        col_chunk(k).start()
        return carry

    lax.fori_loop(0, n_steps, start_wd, 0)
    gate_act[...] = jnp.zeros(gate_act.shape, gate_act.dtype)
    up_act[...] = jnp.zeros(up_act.shape, up_act.dtype)

    def proj_body(k, carry):
        kk = pl.multiple_of(k * step, step)
        x_blk = x_ref[:, pl.ds(kk, step)]
        row_chunk(0, k).wait()
        gate_act[...] += jnp.dot(x_blk, wg[pl.ds(kk, step), :], preferred_element_type=jnp.float32)
        row_chunk(1, k).wait()
        up_act[...] += jnp.dot(x_blk, wu[pl.ds(kk, step), :], preferred_element_type=jnp.float32)
        return carry

    lax.fori_loop(0, n_steps, proj_body, 0)
    hidden_grad[...] = jnp.zeros(hidden_grad.shape, hidden_grad.dtype)

    def hg_body(k, carry):
        kk = pl.multiple_of(k * step, step)
        col_chunk(k).wait()
        hidden_grad[...] += lax.dot_general(
            dy_ref[:, pl.ds(kk, step)], wd[:, pl.ds(kk, step)], nt,
            preferred_element_type=jnp.float32,
        )
        return carry

    lax.fori_loop(0, n_steps, hg_body, 0)
    g = gate_act[...]
    u = up_act[...]
    hg = hidden_grad[...]
    sig = 1.0 / (1.0 + jnp.exp(-g))
    hidden = (g * sig * u).astype(jnp.bfloat16)
    gate_grad = (hg * u * sig * (1.0 + g * (1.0 - sig))).astype(jnp.bfloat16)
    up_grad = (hg * g * sig).astype(jnp.bfloat16)
    hidden_t = jnp.transpose(hidden.astype(jnp.float32)).astype(jnp.bfloat16)

    for c in range(n_steps):
        cc = c * step
        rg = (
            lax.dot_general(gate_grad, wg[cc:cc + step, :], nt, preferred_element_type=jnp.float32)
            + lax.dot_general(up_grad, wu[cc:cc + step, :], nt, preferred_element_type=jnp.float32)
        ).astype(jnp.bfloat16)
        for q in range(step // lane):
            j, h = divmod(cc + q * lane, piece)
            wide[h // lane, pl.ds(j, n_rows, stride=blocks), :] = (
                rg[:, q * lane:(q + 1) * lane].astype(jnp.float32)
            )
        slot = c % 2
        if c >= 2:
            pltpu.make_async_copy(
                down_buf.at[slot], down_hbm.at[:, cc - 2 * step:cc - step], osem.at[slot]
            ).wait()
        down_buf[slot] = jnp.dot(
            hidden_t, dy_ref[:, cc:cc + step], preferred_element_type=jnp.float32
        ).astype(down_buf.dtype)
        pltpu.make_async_copy(down_buf.at[slot], down_hbm.at[:, cc:cc + step], osem.at[slot]).start()
    for cb in range(wide.shape[0]):
        row_out[:, cb * lane:(cb + 1) * lane] = wide[cb].astype(row_out.dtype)
    for c in (n_steps - 2, n_steps - 1):
        pltpu.make_async_copy(
            down_buf.at[c % 2], down_hbm.at[:, c * step:(c + 1) * step], osem.at[c % 2]
        ).wait()


def expert_math(x_flat, dy_flat, w_gate_e, w_up_e, w_down_e, n_rows, width):
    hid = w_gate_e.shape[1]
    vmem = pl.BlockSpec(memory_space=pltpu.VMEM)
    hbm = pl.BlockSpec(memory_space=pl.ANY)
    row_flat, down_local = pl.pallas_call(
        _expert_kernel,
        out_shape=[
            jax.ShapeDtypeStruct(x_flat.shape, jnp.bfloat16),
            jax.ShapeDtypeStruct((hid, width), jnp.bfloat16),
        ],
        in_specs=[vmem, vmem, hbm, hbm, hbm],
        out_specs=[vmem, hbm],
        scratch_shapes=[
            pltpu.VMEM(w_gate_e.shape, w_gate_e.dtype),
            pltpu.VMEM(w_up_e.shape, w_up_e.dtype),
            pltpu.VMEM(w_down_e.shape, w_down_e.dtype),
            pltpu.VMEM((n_rows, hid), jnp.float32),
            pltpu.VMEM((n_rows, hid), jnp.float32),
            pltpu.VMEM((n_rows, hid), jnp.float32),
            pltpu.VMEM((2, hid, 2048), jnp.bfloat16),
            pltpu.VMEM((n_rows, width), jnp.bfloat16),
            pltpu.VMEM((n_rows, width), jnp.bfloat16),
            pltpu.VMEM((x_flat.shape[1] // 128, x_flat.shape[0], 128), jnp.float32),
            pltpu.SemaphoreType.DMA((3, width // 2048)),
            pltpu.SemaphoreType.DMA((2,)),
        ],
        compiler_params=pltpu.CompilerParams(vmem_limit_bytes=62 * 1024 * 1024),
    )(x_flat, dy_flat, w_gate_e, w_up_e, w_down_e)
    return (down_local, row_flat)


def body(
    tokens, out_grad, node_lists, expert_local, gate_fixed, gate_weight, up_weight, down_weight
):
    nodes = lax.axis_size("node")
    per_node = lax.axis_size("local")
    experts = nodes * per_node
    tok_dev, top_count = expert_local.shape
    width = tokens.shape[1]
    capacity = tok_dev * top_count // experts
    group_pos = expert_local // per_node
    node_pick = jnp.zeros_like(expert_local)
    for k in range(node_lists.shape[1]):
        node_pick = node_pick + jnp.where(group_pos == k, node_lists[:, k:k + 1], 0)
    expert_ids = (node_pick * per_node + expert_local % per_node).reshape(-1)
    onehot = (expert_ids[:, None] == jnp.arange(experts, dtype=jnp.int32)[None, :]).astype(
        jnp.int32
    )
    running = jnp.cumsum(onehot, axis=0)
    slot = jnp.sum(onehot * running, axis=1) - 1
    kept = slot < capacity
    position = jnp.where(kept, expert_ids * capacity + slot, experts * capacity)
    w_gate_e = gate_weight[0]
    w_up_e = up_weight[0]
    w_down_e = down_weight[0]
    gate_flat = gate_fixed.reshape(-1)
    fills = position[:, None] == jnp.arange(experts * capacity, dtype=jnp.int32)[None, :]
    valid = jnp.any(fills, axis=0)
    assign_ids = jnp.arange(tok_dev * top_count, dtype=jnp.int32)[:, None]
    rows = jnp.sum(jnp.where(fills, assign_ids // top_count, 0), axis=0)
    gate_slot = jnp.sum(jnp.where(fills, gate_flat[:, None], 0), axis=0)
    tile_rows = 8
    blocks = tile_rows // capacity
    piece = width // blocks
    slot_token = jnp.where(valid, rows, -1)
    row_key = jnp.where(
        jnp.repeat(valid, blocks),
        jnp.repeat(slot_token, blocks) * blocks + jnp.arange(experts * tile_rows, dtype=jnp.int32) % blocks,
        -1,
    )
    select = (
        row_key[:, None] == jnp.arange(tok_dev * blocks, dtype=jnp.int32)[None, :]
    ).astype(jnp.bfloat16)
    tok_pieces = tokens.reshape(tok_dev * blocks, piece)
    og_pieces = out_grad.reshape(tok_dev * blocks, piece)
    gate_val = jnp.where(valid, gate_slot.astype(jnp.float32) * (1.0 / 65536.0), 0.0)
    gate_rows = jnp.repeat(gate_val, blocks)
    both = jnp.dot(
        select, jnp.concatenate([tok_pieces, og_pieces], axis=1), preferred_element_type=jnp.float32
    )
    send_x = both[:, :piece].astype(jnp.bfloat16)
    send_dy = (gate_rows[:, None] * both[:, piece:]).astype(jnp.bfloat16)
    x_flat, dy_flat = exchange(send_x, send_dy)
    down_local, row_flat = expert_math(
        x_flat, dy_flat, w_gate_e, w_up_e, w_down_e, experts * capacity, width
    )
    (returned,) = exchange(row_flat)
    total = jnp.dot(select.T, returned, preferred_element_type=jnp.float32)
    token_grad = total.reshape(tok_dev, width).astype(jnp.bfloat16)
    return (token_grad, down_local[None])


def solution(mesh):
    return jax.shard_map(
        body,
        mesh=mesh,
        in_specs=(
            P(("node", "local"), None),
            P(("node", "local"), None),
            P(("node", "local"), None),
            P(("node", "local"), None),
            P(("node", "local"), None),
            P(("node", "local"), None, None),
            P(("node", "local"), None, None),
            P(("node", "local"), None, None),
        ),
        out_specs=(P(("node", "local"), None), P(("node", "local"), None, None)),
        check_vma=False,
    )
```

```python
import functools
import jax
import jax.numpy as jnp
from jax import lax
from jax.sharding import PartitionSpec as P
from jax.experimental import pallas as pl
from jax.experimental.pallas import tpu as pltpu


def _exchange_kernel(n_local, *refs):
    count = (len(refs) - 2) // 2
    srcs = refs[:count]
    dsts = refs[count:2 * count]
    send_sems = refs[2 * count]
    recv_sems = refs[2 * count + 1]
    node = lax.axis_index("node")
    local = lax.axis_index("local")
    me = node * n_local + local
    devices = lax.axis_size("node") * n_local
    rows = srcs[0].shape[0] // devices

    def copy_to(p, i):
        return pltpu.make_async_remote_copy(
            src_ref=srcs[i].at[pl.ds(p * rows, rows)],
            dst_ref=dsts[i].at[pl.ds(me * rows, rows)],
            send_sem=send_sems.at[i],
            recv_sem=recv_sems.at[i],
            device_id=(p // n_local, p % n_local),
            device_id_type=pl.DeviceIdType.MESH,
        )

    def local_copy(i):
        return pltpu.make_async_copy(
            srcs[i].at[pl.ds(me * rows, rows)],
            dsts[i].at[pl.ds(me * rows, rows)],
            recv_sems.at[i],
        )

    for i in range(count):
        local_copy(i).start()

    core = node % 2
    y_pos = (node // 2) % 4
    z_pos = node // 8

    def start_body(step, carry):
        t = step % 64
        d_core = step // 64
        dx = t % 4
        dy = (t // 4 + dx) % 4
        dz = (t // 16 + t // 4 + dx) % 4
        node_to = (((z_pos + dz) % 4) * 4 + (y_pos + dy) % 4) * 2 + (core + d_core) % 2
        p = node_to * n_local + (local + dx) % 4
        for i in range(count):
            copy_to(p, i).start()
        return carry

    lax.fori_loop(1, devices, start_body, 0)
    nxt = lax.rem(me + 1, devices)
    for i in range(count):
        pltpu.make_async_copy(dsts[i], dsts[i], recv_sems.at[i]).wait()
        pltpu.make_async_remote_copy(
            src_ref=srcs[i].at[pl.ds(0, (devices - 1) * rows)],
            dst_ref=dsts[i].at[pl.ds(0, (devices - 1) * rows)],
            send_sem=send_sems.at[i],
            recv_sem=recv_sems.at[i],
            device_id=(nxt // n_local, nxt % n_local),
            device_id_type=pl.DeviceIdType.MESH,
        ).wait_send()


def exchange(*arrays):
    n_local = lax.axis_size("local")
    count = len(arrays)
    return pl.pallas_call(
        functools.partial(_exchange_kernel, n_local),
        out_shape=[jax.ShapeDtypeStruct(a.shape, a.dtype) for a in arrays],
        in_specs=[pl.BlockSpec(memory_space=pl.ANY)] * count,
        out_specs=[pl.BlockSpec(memory_space=pl.ANY)] * count,
        scratch_shapes=[
            pltpu.SemaphoreType.DMA((count,)),
            pltpu.SemaphoreType.DMA((count,)),
        ],
        compiler_params=pltpu.CompilerParams(has_side_effects=True),
    )(*arrays)


def _expert_kernel(xf_ref, dyf_ref, wg_hbm, wu_hbm, wd_hbm, row_out, down_hbm,
                   wg, wu, wd, gate_act, up_act, hidden_grad, down_buf, x_ref, dy_ref, wide,
                   wsem, osem):
    k_total = x_ref.shape[1]
    lane = wide.shape[2]
    n_rows = x_ref.shape[0]
    blocks = wide.shape[1] // n_rows
    piece = wide.shape[0] * lane
    for src, dst in ((xf_ref, x_ref), (dyf_ref, dy_ref)):
        for cb in range(wide.shape[0]):
            wide[cb] = src[:, cb * lane:(cb + 1) * lane].astype(jnp.float32)
        for j in range(blocks):
            for cb in range(wide.shape[0]):
                col = j * piece + cb * lane
                dst[:, col:col + lane] = wide[cb, pl.ds(j, n_rows, stride=blocks), :].astype(dst.dtype)
    step = 4096
    n_steps = k_total // step
    nt = (((1,), (1,)), ((), ()))
    sources = ((wg_hbm, wg), (wu_hbm, wu))

    def row_chunk(i, k):
        src, dst = sources[i]
        kk = pl.multiple_of(k * step, step)
        return pltpu.make_async_copy(src.at[pl.ds(kk, step)], dst.at[pl.ds(kk, step)], wsem.at[i, k])

    def col_chunk(k):
        kk = pl.multiple_of(k * step, step)
        return pltpu.make_async_copy(wd_hbm.at[:, pl.ds(kk, step)], wd.at[:, pl.ds(kk, step)], wsem.at[2, k])

    def start_body(k, carry):
        row_chunk(0, k).start()
        row_chunk(1, k).start()
        return carry

    lax.fori_loop(0, n_steps, start_body, 0)

    def start_wd(k, carry):
        col_chunk(k).start()
        return carry

    lax.fori_loop(0, n_steps, start_wd, 0)
    gate_act[...] = jnp.zeros(gate_act.shape, gate_act.dtype)
    up_act[...] = jnp.zeros(up_act.shape, up_act.dtype)

    def proj_body(k, carry):
        kk = pl.multiple_of(k * step, step)
        x_blk = x_ref[:, pl.ds(kk, step)]
        row_chunk(0, k).wait()
        gate_act[...] += jnp.dot(x_blk, wg[pl.ds(kk, step), :], preferred_element_type=jnp.float32)
        row_chunk(1, k).wait()
        up_act[...] += jnp.dot(x_blk, wu[pl.ds(kk, step), :], preferred_element_type=jnp.float32)
        return carry

    lax.fori_loop(0, n_steps, proj_body, 0)
    hidden_grad[...] = jnp.zeros(hidden_grad.shape, hidden_grad.dtype)

    def hg_body(k, carry):
        kk = pl.multiple_of(k * step, step)
        col_chunk(k).wait()
        hidden_grad[...] += lax.dot_general(
            dy_ref[:, pl.ds(kk, step)], wd[:, pl.ds(kk, step)], nt,
            preferred_element_type=jnp.float32,
        )
        return carry

    lax.fori_loop(0, n_steps, hg_body, 0)
    g = gate_act[...]
    u = up_act[...]
    hg = hidden_grad[...]
    sig = 1.0 / (1.0 + jnp.exp(-g))
    hidden = (g * sig * u).astype(jnp.bfloat16)
    gate_grad = (hg * u * sig * (1.0 + g * (1.0 - sig))).astype(jnp.bfloat16)
    up_grad = (hg * g * sig).astype(jnp.bfloat16)
    hidden_t = jnp.transpose(hidden.astype(jnp.float32)).astype(jnp.bfloat16)

    for c in range(n_steps):
        cc = c * step
        rg = (
            lax.dot_general(gate_grad, wg[cc:cc + step, :], nt, preferred_element_type=jnp.float32)
            + lax.dot_general(up_grad, wu[cc:cc + step, :], nt, preferred_element_type=jnp.float32)
        ).astype(jnp.bfloat16)
        for q in range(step // lane):
            j, h = divmod(cc + q * lane, piece)
            wide[h // lane, pl.ds(j, n_rows, stride=blocks), :] = (
                rg[:, q * lane:(q + 1) * lane].astype(jnp.float32)
            )
        slot = c % 2
        if c >= 2:
            pltpu.make_async_copy(
                down_buf.at[slot], down_hbm.at[:, cc - 2 * step:cc - step], osem.at[slot]
            ).wait()
        down_buf[slot] = jnp.dot(
            hidden_t, dy_ref[:, cc:cc + step], preferred_element_type=jnp.float32
        ).astype(down_buf.dtype)
        pltpu.make_async_copy(down_buf.at[slot], down_hbm.at[:, cc:cc + step], osem.at[slot]).start()
    for cb in range(wide.shape[0]):
        row_out[:, cb * lane:(cb + 1) * lane] = wide[cb].astype(row_out.dtype)
    for c in range(max(0, n_steps - 2), n_steps):
        pltpu.make_async_copy(
            down_buf.at[c % 2], down_hbm.at[:, c * step:(c + 1) * step], osem.at[c % 2]
        ).wait()


def expert_math(x_flat, dy_flat, w_gate_e, w_up_e, w_down_e, n_rows, width):
    hid = w_gate_e.shape[1]
    vmem = pl.BlockSpec(memory_space=pltpu.VMEM)
    hbm = pl.BlockSpec(memory_space=pl.ANY)
    row_flat, down_local = pl.pallas_call(
        _expert_kernel,
        out_shape=[
            jax.ShapeDtypeStruct(x_flat.shape, jnp.bfloat16),
            jax.ShapeDtypeStruct((hid, width), jnp.bfloat16),
        ],
        in_specs=[vmem, vmem, hbm, hbm, hbm],
        out_specs=[vmem, hbm],
        scratch_shapes=[
            pltpu.VMEM(w_gate_e.shape, w_gate_e.dtype),
            pltpu.VMEM(w_up_e.shape, w_up_e.dtype),
            pltpu.VMEM(w_down_e.shape, w_down_e.dtype),
            pltpu.VMEM((n_rows, hid), jnp.float32),
            pltpu.VMEM((n_rows, hid), jnp.float32),
            pltpu.VMEM((n_rows, hid), jnp.float32),
            pltpu.VMEM((2, hid, 4096), jnp.bfloat16),
            pltpu.VMEM((n_rows, width), jnp.bfloat16),
            pltpu.VMEM((n_rows, width), jnp.bfloat16),
            pltpu.VMEM((x_flat.shape[1] // 128, x_flat.shape[0], 128), jnp.float32),
            pltpu.SemaphoreType.DMA((3, width // 4096)),
            pltpu.SemaphoreType.DMA((2,)),
        ],
        compiler_params=pltpu.CompilerParams(vmem_limit_bytes=62 * 1024 * 1024),
    )(x_flat, dy_flat, w_gate_e, w_up_e, w_down_e)
    return (down_local, row_flat)


def body(
    tokens, out_grad, node_lists, expert_local, gate_fixed, gate_weight, up_weight, down_weight
):
    nodes = lax.axis_size("node")
    per_node = lax.axis_size("local")
    experts = nodes * per_node
    tok_dev, top_count = expert_local.shape
    width = tokens.shape[1]
    capacity = tok_dev * top_count // experts
    group_pos = expert_local // per_node
    node_pick = jnp.zeros_like(expert_local)
    for k in range(node_lists.shape[1]):
        node_pick = node_pick + jnp.where(group_pos == k, node_lists[:, k:k + 1], 0)
    expert_ids = (node_pick * per_node + expert_local % per_node).reshape(-1)
    onehot = (expert_ids[:, None] == jnp.arange(experts, dtype=jnp.int32)[None, :]).astype(
        jnp.int32
    )
    running = jnp.cumsum(onehot, axis=0)
    slot = jnp.sum(onehot * running, axis=1) - 1
    kept = slot < capacity
    position = jnp.where(kept, expert_ids * capacity + slot, experts * capacity)
    w_gate_e = gate_weight[0]
    w_up_e = up_weight[0]
    w_down_e = down_weight[0]
    gate_flat = gate_fixed.reshape(-1)
    fills = position[:, None] == jnp.arange(experts * capacity, dtype=jnp.int32)[None, :]
    valid = jnp.any(fills, axis=0)
    assign_ids = jnp.arange(tok_dev * top_count, dtype=jnp.int32)[:, None]
    rows = jnp.sum(jnp.where(fills, assign_ids // top_count, 0), axis=0)
    gate_slot = jnp.sum(jnp.where(fills, gate_flat[:, None], 0), axis=0)
    tile_rows = 8
    blocks = tile_rows // capacity
    piece = width // blocks
    slot_token = jnp.where(valid, rows, -1)
    row_key = jnp.where(
        jnp.repeat(valid, blocks),
        jnp.repeat(slot_token, blocks) * blocks + jnp.arange(experts * tile_rows, dtype=jnp.int32) % blocks,
        -1,
    )
    select = (
        row_key[:, None] == jnp.arange(tok_dev * blocks, dtype=jnp.int32)[None, :]
    ).astype(jnp.bfloat16)
    tok_pieces = tokens.reshape(tok_dev * blocks, piece)
    og_pieces = out_grad.reshape(tok_dev * blocks, piece)
    send_x = jnp.dot(select, tok_pieces, preferred_element_type=jnp.float32).astype(jnp.bfloat16)
    gate_val = jnp.where(valid, gate_slot.astype(jnp.float32) * (1.0 / 65536.0), 0.0)
    gate_rows = jnp.repeat(gate_val, blocks)
    og_sel = jnp.dot(select, og_pieces, preferred_element_type=jnp.float32)
    send_dy = (gate_rows[:, None] * og_sel).astype(jnp.bfloat16)
    x_flat, dy_flat = exchange(send_x, send_dy)
    down_local, row_flat = expert_math(
        x_flat, dy_flat, w_gate_e, w_up_e, w_down_e, experts * capacity, width
    )
    (returned,) = exchange(row_flat)
    total = jnp.dot(select.T, returned, preferred_element_type=jnp.float32)
    token_grad = total.reshape(tok_dev, width).astype(jnp.bfloat16)
    return (token_grad, down_local[None])


def solution(mesh):
    return jax.shard_map(
        body,
        mesh=mesh,
        in_specs=(
            P(("node", "local"), None),
            P(("node", "local"), None),
            P(("node", "local"), None),
            P(("node", "local"), None),
            P(("node", "local"), None),
            P(("node", "local"), None, None),
            P(("node", "local"), None, None),
            P(("node", "local"), None, None),
        ),
        out_specs=(P(("node", "local"), None), P(("node", "local"), None, None)),
        check_vma=False,
    )
```

```python
import functools
import jax
import jax.numpy as jnp
from jax import lax
from jax.sharding import PartitionSpec as P
from jax.experimental import pallas as pl
from jax.experimental.pallas import tpu as pltpu


def _exchange_kernel(n_local, *refs):
    count = (len(refs) - 2) // 2
    srcs = refs[:count]
    dsts = refs[count:2 * count]
    send_sems = refs[2 * count]
    recv_sems = refs[2 * count + 1]
    node = lax.axis_index("node")
    local = lax.axis_index("local")
    me = node * n_local + local
    devices = lax.axis_size("node") * n_local
    rows = srcs[0].shape[0] // devices

    def copy_to(p, i):
        return pltpu.make_async_remote_copy(
            src_ref=srcs[i].at[pl.ds(p * rows, rows)],
            dst_ref=dsts[i].at[pl.ds(me * rows, rows)],
            send_sem=send_sems.at[i],
            recv_sem=recv_sems.at[i],
            device_id=(p // n_local, p % n_local),
            device_id_type=pl.DeviceIdType.MESH,
        )

    def local_copy(i):
        return pltpu.make_async_copy(
            srcs[i].at[pl.ds(me * rows, rows)],
            dsts[i].at[pl.ds(me * rows, rows)],
            recv_sems.at[i],
        )

    for i in range(count):
        local_copy(i).start()

    core = node % 2
    y_pos = (node // 2) % 4
    z_pos = node // 8

    def start_body(step, carry):
        t = step % 64
        d_core = step // 64
        dx = t % 4
        dy = (t // 4 + dx) % 4
        dz = (t // 16 + t // 4 + dx) % 4
        node_to = (((z_pos + dz) % 4) * 4 + (y_pos + dy) % 4) * 2 + (core + d_core) % 2
        p = node_to * n_local + (local + dx) % 4
        for i in range(count):
            copy_to(p, i).start()
        return carry

    lax.fori_loop(1, devices, start_body, 0)
    nxt = lax.rem(me + 1, devices)
    for i in range(count):
        pltpu.make_async_copy(dsts[i], dsts[i], recv_sems.at[i]).wait()
        pltpu.make_async_remote_copy(
            src_ref=srcs[i].at[pl.ds(0, (devices - 1) * rows)],
            dst_ref=dsts[i].at[pl.ds(0, (devices - 1) * rows)],
            send_sem=send_sems.at[i],
            recv_sem=recv_sems.at[i],
            device_id=(nxt // n_local, nxt % n_local),
            device_id_type=pl.DeviceIdType.MESH,
        ).wait_send()


def exchange(*arrays):
    n_local = lax.axis_size("local")
    count = len(arrays)
    return pl.pallas_call(
        functools.partial(_exchange_kernel, n_local),
        out_shape=[jax.ShapeDtypeStruct(a.shape, a.dtype) for a in arrays],
        in_specs=[pl.BlockSpec(memory_space=pl.ANY)] * count,
        out_specs=[pl.BlockSpec(memory_space=pl.ANY)] * count,
        scratch_shapes=[
            pltpu.SemaphoreType.DMA((count,)),
            pltpu.SemaphoreType.DMA((count,)),
        ],
        compiler_params=pltpu.CompilerParams(has_side_effects=True),
    )(*arrays)


def _expert_kernel(xf_ref, dyf_ref, wg_hbm, wu_hbm, wd_hbm, row_out, down_hbm,
                   wg, wu, wd, gate_act, up_act, hidden_grad, down_buf, x_ref, dy_ref, wide,
                   wsem, osem):
    k_total = x_ref.shape[1]
    lane = wide.shape[2]
    n_rows = x_ref.shape[0]
    blocks = wide.shape[1] // n_rows
    piece = wide.shape[0] * lane
    for src, dst in ((xf_ref, x_ref), (dyf_ref, dy_ref)):
        for cb in range(wide.shape[0]):
            wide[cb] = src[:, cb * lane:(cb + 1) * lane].astype(jnp.float32)
        for j in range(blocks):
            for cb in range(wide.shape[0]):
                col = j * piece + cb * lane
                dst[:, col:col + lane] = wide[cb, pl.ds(j, n_rows, stride=blocks), :].astype(dst.dtype)
    step = 2048
    n_steps = k_total // step
    nt = (((1,), (1,)), ((), ()))
    sources = ((wg_hbm, wg), (wu_hbm, wu))

    def row_chunk(i, k):
        src, dst = sources[i]
        kk = pl.multiple_of(k * step, step)
        return pltpu.make_async_copy(src.at[pl.ds(kk, step)], dst.at[pl.ds(kk, step)], wsem.at[i, k])

    def col_chunk(k):
        kk = pl.multiple_of(k * step, step)
        return pltpu.make_async_copy(wd_hbm.at[:, pl.ds(kk, step)], wd.at[:, pl.ds(kk, step)], wsem.at[2, k])

    def start_body(k, carry):
        row_chunk(0, k).start()
        row_chunk(1, k).start()
        return carry

    lax.fori_loop(0, n_steps, start_body, 0)

    def start_wd(k, carry):
        col_chunk(k).start()
        return carry

    lax.fori_loop(0, n_steps, start_wd, 0)
    gate_act[...] = jnp.zeros(gate_act.shape, gate_act.dtype)
    up_act[...] = jnp.zeros(up_act.shape, up_act.dtype)

    def proj_body(k, carry):
        kk = pl.multiple_of(k * step, step)
        x_blk = x_ref[:, pl.ds(kk, step)]
        row_chunk(0, k).wait()
        gate_act[...] += jnp.dot(x_blk, wg[pl.ds(kk, step), :], preferred_element_type=jnp.float32)
        row_chunk(1, k).wait()
        up_act[...] += jnp.dot(x_blk, wu[pl.ds(kk, step), :], preferred_element_type=jnp.float32)
        return carry

    lax.fori_loop(0, n_steps, proj_body, 0)
    hidden_grad[...] = jnp.zeros(hidden_grad.shape, hidden_grad.dtype)

    def hg_body(k, carry):
        kk = pl.multiple_of(k * step, step)
        col_chunk(k).wait()
        hidden_grad[...] += lax.dot_general(
            dy_ref[:, pl.ds(kk, step)], wd[:, pl.ds(kk, step)], nt,
            preferred_element_type=jnp.float32,
        )
        return carry

    lax.fori_loop(0, n_steps, hg_body, 0)
    g = gate_act[...]
    u = up_act[...]
    hg = hidden_grad[...]
    sig = 1.0 / (1.0 + jnp.exp(-g))
    hidden = (g * sig * u).astype(jnp.bfloat16)
    gate_grad = (hg * u * sig * (1.0 + g * (1.0 - sig))).astype(jnp.bfloat16)
    up_grad = (hg * g * sig).astype(jnp.bfloat16)
    hidden_t = jnp.transpose(hidden.astype(jnp.float32)).astype(jnp.bfloat16)

    for c in range(n_steps):
        cc = c * step
        rg = (
            lax.dot_general(gate_grad, wg[cc:cc + step, :], nt, preferred_element_type=jnp.float32)
            + lax.dot_general(up_grad, wu[cc:cc + step, :], nt, preferred_element_type=jnp.float32)
        ).astype(jnp.bfloat16)
        for q in range(step // lane):
            j, h = divmod(cc + q * lane, piece)
            wide[h // lane, pl.ds(j, n_rows, stride=blocks), :] = (
                rg[:, q * lane:(q + 1) * lane].astype(jnp.float32)
            )
        slot = c % 2
        if c >= 2:
            pltpu.make_async_copy(
                down_buf.at[slot], down_hbm.at[:, cc - 2 * step:cc - step], osem.at[slot]
            ).wait()
        down_buf[slot] = jnp.dot(
            hidden_t, dy_ref[:, cc:cc + step], preferred_element_type=jnp.float32
        ).astype(down_buf.dtype)
        pltpu.make_async_copy(down_buf.at[slot], down_hbm.at[:, cc:cc + step], osem.at[slot]).start()
    for cb in range(wide.shape[0]):
        row_out[:, cb * lane:(cb + 1) * lane] = wide[cb].astype(row_out.dtype)
    for c in (n_steps - 2, n_steps - 1):
        pltpu.make_async_copy(
            down_buf.at[c % 2], down_hbm.at[:, c * step:(c + 1) * step], osem.at[c % 2]
        ).wait()


def expert_math(x_flat, dy_flat, w_gate_e, w_up_e, w_down_e, n_rows, width):
    hid = w_gate_e.shape[1]
    vmem = pl.BlockSpec(memory_space=pltpu.VMEM)
    hbm = pl.BlockSpec(memory_space=pl.ANY)
    row_flat, down_local = pl.pallas_call(
        _expert_kernel,
        out_shape=[
            jax.ShapeDtypeStruct(x_flat.shape, jnp.bfloat16),
            jax.ShapeDtypeStruct((hid, width), jnp.bfloat16),
        ],
        in_specs=[vmem, vmem, hbm, hbm, hbm],
        out_specs=[vmem, hbm],
        scratch_shapes=[
            pltpu.VMEM(w_gate_e.shape, w_gate_e.dtype),
            pltpu.VMEM(w_up_e.shape, w_up_e.dtype),
            pltpu.VMEM(w_down_e.shape, w_down_e.dtype),
            pltpu.VMEM((n_rows, hid), jnp.float32),
            pltpu.VMEM((n_rows, hid), jnp.float32),
            pltpu.VMEM((n_rows, hid), jnp.float32),
            pltpu.VMEM((2, hid, 2048), jnp.bfloat16),
            pltpu.VMEM((n_rows, width), jnp.bfloat16),
            pltpu.VMEM((n_rows, width), jnp.bfloat16),
            pltpu.VMEM((x_flat.shape[1] // 128, x_flat.shape[0], 128), jnp.float32),
            pltpu.SemaphoreType.DMA((3, width // 2048)),
            pltpu.SemaphoreType.DMA((2,)),
        ],
        compiler_params=pltpu.CompilerParams(vmem_limit_bytes=62 * 1024 * 1024),
    )(x_flat, dy_flat, w_gate_e, w_up_e, w_down_e)
    return (down_local, row_flat)


def body(
    tokens, out_grad, node_lists, expert_local, gate_fixed, gate_weight, up_weight, down_weight
):
    nodes = lax.axis_size("node")
    per_node = lax.axis_size("local")
    experts = nodes * per_node
    tok_dev, top_count = expert_local.shape
    width = tokens.shape[1]
    capacity = tok_dev * top_count // experts
    group_pos = expert_local // per_node
    node_pick = jnp.zeros_like(expert_local)
    for k in range(node_lists.shape[1]):
        node_pick = node_pick + jnp.where(group_pos == k, node_lists[:, k:k + 1], 0)
    expert_ids = (node_pick * per_node + expert_local % per_node).reshape(-1)
    onehot = (expert_ids[:, None] == jnp.arange(experts, dtype=jnp.int32)[None, :]).astype(
        jnp.int32
    )
    running = jnp.cumsum(onehot, axis=0)
    slot = jnp.sum(onehot * running, axis=1) - 1
    kept = slot < capacity
    position = jnp.where(kept, expert_ids * capacity + slot, experts * capacity)
    w_gate_e = gate_weight[0]
    w_up_e = up_weight[0]
    w_down_e = down_weight[0]
    gate_flat = gate_fixed.reshape(-1)
    fills = position[:, None] == jnp.arange(experts * capacity, dtype=jnp.int32)[None, :]
    valid = jnp.any(fills, axis=0)
    assign_ids = jnp.arange(tok_dev * top_count, dtype=jnp.int32)[:, None]
    rows = jnp.sum(jnp.where(fills, assign_ids // top_count, 0), axis=0)
    gate_slot = jnp.sum(jnp.where(fills, gate_flat[:, None], 0), axis=0)
    tile_rows = 8
    blocks = tile_rows // capacity
    piece = width // blocks
    slot_token = jnp.where(valid, rows, -1)
    row_key = jnp.where(
        jnp.repeat(valid, blocks),
        jnp.repeat(slot_token, blocks) * blocks + jnp.arange(experts * tile_rows, dtype=jnp.int32) % blocks,
        -1,
    )
    select = (
        row_key[:, None] == jnp.arange(tok_dev * blocks, dtype=jnp.int32)[None, :]
    ).astype(jnp.bfloat16)
    tok_pieces = tokens.reshape(tok_dev * blocks, piece)
    og_pieces = out_grad.reshape(tok_dev * blocks, piece)
    send_x = jnp.dot(select, tok_pieces, preferred_element_type=jnp.float32).astype(jnp.bfloat16)
    gate_val = jnp.where(valid, gate_slot.astype(jnp.float32) * (1.0 / 65536.0), 0.0)
    gate_rows = jnp.repeat(gate_val, blocks)
    og_sel = jnp.dot(select, og_pieces, preferred_element_type=jnp.float32)
    send_dy = (gate_rows[:, None] * og_sel).astype(jnp.bfloat16)
    x_flat, dy_flat = exchange(send_x, send_dy)
    down_local, row_flat = expert_math(
        x_flat, dy_flat, w_gate_e, w_up_e, w_down_e, experts * capacity, width
    )
    (returned,) = exchange(row_flat)
    gather_t = select.T
    token_grad = jnp.concatenate(
        [
            jnp.dot(gather_t[j::blocks], returned, preferred_element_type=jnp.float32)
            for j in range(blocks)
        ],
        axis=1,
    ).astype(jnp.bfloat16)
    return (token_grad, down_local[None])


def solution(mesh):
    return jax.shard_map(
        body,
        mesh=mesh,
        in_specs=(
            P(("node", "local"), None),
            P(("node", "local"), None),
            P(("node", "local"), None),
            P(("node", "local"), None),
            P(("node", "local"), None),
            P(("node", "local"), None, None),
            P(("node", "local"), None, None),
            P(("node", "local"), None, None),
        ),
        out_specs=(P(("node", "local"), None), P(("node", "local"), None, None)),
        check_vma=False,
    )
```
